512 devices in a mesh: chan: 128 (over z, y, core), orb: 4 (over x).
Axes of the slice: x: 4, y: 8, z: 8, core: 2. Of those that a mesh axis runs over, the one named last changes fastest.
Arguments:
- amplitudes: bfloat16 [327680, 1024], P(('chan', 'orb')), may hold values from -6 to 6
- recoupling: float32 [327680], P(('chan', 'orb')), may hold values from -1.5 to 1.5
- denominators: float32 [327680], P(('chan', 'orb')), may hold values from 1 to 8
- interaction: bfloat16 [512, 1024, 1024], P('chan', 'orb'), may hold values from -0.25 to 0.25
- pair_source: int32 [512, 1024], P('chan', 'orb'), may hold values from -1 to 639, as said below
- return_slot: int32 [327680], P(('chan', 'orb')), may hold values from 0 to 1023, as said below
- channel_sizes: int32 [512], P('chan'), may hold values from 256 to 1024, as said below
Outputs:
- updated: bfloat16 [327680, 1024], P(('chan', 'orb'))
The draws below stay inside these ranges and needn't reach their ends.
Inputs may be any that keep to these rules, and one draw needn't show every extreme that they name: `channel_sizes`: every channel size is a multiple of 4; the 4 sizes of blocks c with the same c div 4 sum to 2560. pair_source[c, p] = -1 exactly where live[c, p] = 0. For each e and o, over the blocks c with c div 4 = e and the positions p with p div 256 = o, the other values name each number 0 to 639 once. return_slot[(e * 4 + o) * 640 + i] is the k with pair_source[e * 4 + k div 256, o * 256 + k mod 256] = i.
All inputs are finite; a program needn't handle non-finite values.
Results may differ from the reference program's by a relative error of at most 0.002.
Values may be sent and summed in bfloat16 or wider, within the bound.
No kernel may reach another device: no remote copies, remote signals or barrier semaphores. Data moves between devices by JAX's collectives and lax.ppermute only.
A program may use at most 64 MiB of HBM per device.

```python
import math
import jax
import jax.numpy as jnp
from jax import lax

B = 1024
BLK_DEV = 4
MEAN_SIZE = 640
ROWS_BLOCK = 256
P_DEV = 640
QUOTA = 5
NB = 512
PP_ROWS = 327680
N_CHAN = 128
N_ORB = 4


def layout(key):
    size_key, perm_key = jax.random.split(jax.random.fold_in(key, 11))
    chan_total = NB // BLK_DEV
    orb_total = B // ROWS_BLOCK
    spread = (B - MEAN_SIZE) // orb_total
    half_shift = jax.random.randint(size_key, (chan_total, BLK_DEV // 2), -spread, spread + 1)
    half_shift = half_shift.at[0, 0].set(spread)
    half_shift = half_shift.at[0, BLK_DEV // 2 - 1].set(-spread)
    block_sizes = jnp.stack([MEAN_SIZE + orb_total * half_shift, MEAN_SIZE - orb_total * half_shift], axis=2)
    block_sizes = block_sizes.reshape(chan_total, BLK_DEV).astype(jnp.int32)
    column_ids = jnp.arange(ROWS_BLOCK, dtype=jnp.int32)
    orb_ids = jnp.arange(orb_total, dtype=jnp.int32)
    pair_rank = orb_total * column_ids[None, :] + orb_ids[:, None]
    live_mask = pair_rank[None, :, None, :] < block_sizes[:, None, :, None]
    live_flat = live_mask.reshape(chan_total, orb_total, BLK_DEV * ROWS_BLOCK)
    live_order = jnp.cumsum(live_flat.astype(jnp.int32), axis=2) - 1
    perm_keys = jax.random.split(perm_key, chan_total * orb_total)
    shuffles = jax.vmap(lambda subkey: jax.random.permutation(subkey, P_DEV))(perm_keys)
    shuffles = shuffles.reshape(chan_total, orb_total, P_DEV).astype(jnp.int32)
    picked = jnp.take_along_axis(shuffles, jnp.clip(live_order, 0, P_DEV - 1), axis=2)
    source = jnp.where(live_flat, picked, -1).astype(jnp.int32)
    pair_source = source.reshape(chan_total, orb_total, BLK_DEV, ROWS_BLOCK).transpose(0, 2, 1, 3).reshape(NB, B)
    local_ids = jnp.arange(BLK_DEV * ROWS_BLOCK, dtype=jnp.int32)
    sort_score = jnp.where(live_flat, source, P_DEV + local_ids[None, None, :])
    return_slot = jnp.argsort(sort_score, axis=2, stable=True)[:, :, :P_DEV].reshape(-1).astype(jnp.int32)
    return (block_sizes.reshape(NB), pair_source, return_slot)


def draw_channel_sizes(key, part):
    return layout(key)[0]


def draw_pair_source(key, part):
    return layout(key)[1]


def draw_return_slot(key, part):
    return layout(key)[2]


def block_scale(own_key, extent, shards, least, top_value):
    loudness = 1.0
    for dim, shards_of in shards:
        draws = jax.random.uniform(jax.random.fold_in(jax.random.fold_in(own_key, 6), dim), (shards_of,), jnp.float32, least / len(shards), top_value / len(shards))
        loudness = loudness * jnp.repeat(jnp.exp(draws), extent[dim] // shards_of).reshape((-1,) + (1,) * (len(extent) - 1 - dim))
    return loudness


def normal_values(stream_key, dims, width, most, pieces=(), kind=jnp.bfloat16):
    drawn = jax.random.normal(stream_key, dims, jnp.float32) * width
    if len(pieces) > 0:
        drawn = block_scale(stream_key, dims, pieces, -0.22, 0.18) * drawn
    return jnp.clip(drawn, min=-most, max=most).astype(kind)


def setup_inputs(seed: int = 0) -> dict:
    keys = jax.random.split(jax.random.key(seed), 8)
    return {
        "amplitudes": normal_values(keys[0], (PP_ROWS, B), 1.0, 6.0, ((0, 512),)),
        "recoupling": jnp.clip(jax.random.uniform(keys[1], (PP_ROWS,), jnp.float32, -1.5, 1.5) * block_scale(keys[1], (PP_ROWS,), ((0, 512),), -0.4, 0.0), -1.5, 1.5),
        "denominators": jnp.clip(jnp.exp(math.log(8.0) - 2.0794415 * jax.random.uniform(keys[2], (PP_ROWS,), jnp.float32) ** block_scale(keys[2], (PP_ROWS,), ((0, 512),), -0.2, 0.2)), 1.0, 8.0),
        "interaction": normal_values(keys[3], (NB, B, B), MEAN_SIZE ** -0.5, 0.25, ((0, 128), (1, 4))),
        "pair_source": draw_pair_source(jax.random.fold_in(keys[7], 71), 0),
        "return_slot": draw_return_slot(jax.random.fold_in(keys[7], 71), 0),
        "channel_sizes": draw_channel_sizes(jax.random.fold_in(keys[7], 71), 0),
    }


def reference(amplitudes, recoupling, denominators, interaction, pair_source, return_slot, channel_sizes):
    amp_grid = amplitudes.reshape(N_CHAN, N_ORB, P_DEV, B)
    weight_grid = recoupling.reshape(N_CHAN, N_ORB, P_DEV)
    slot_grid = return_slot.reshape(N_CHAN, N_ORB, P_DEV)
    position = jnp.arange(B, dtype=jnp.int32)
    pair_rank = N_ORB * (position % ROWS_BLOCK) + position // ROWS_BLOCK
    owner_orb = position // ROWS_BLOCK
    orb_ids = jnp.arange(N_ORB, dtype=jnp.int32)

    def per_chan(chan_number):
        offset = (chan_number * QUOTA).astype(jnp.int32)
        sent_amp = lax.dynamic_slice_in_dim(amp_grid, offset, QUOTA, 2)
        sent_weight = lax.dynamic_slice_in_dim(weight_grid, offset, QUOTA, 2)
        relayed = (sent_amp.astype(jnp.float32) * sent_weight[..., None]).astype(jnp.bfloat16)
        received = jnp.transpose(relayed, (1, 0, 2, 3)).reshape(N_ORB * P_DEV, B)
        first_block = (chan_number * BLK_DEV).astype(jnp.int32)
        source = lax.dynamic_slice_in_dim(pair_source, first_block, BLK_DEV, 0)
        block_sizes = lax.dynamic_slice_in_dim(channel_sizes, first_block, BLK_DEV, 0)
        gather_at = owner_orb[None, :] * P_DEV + jnp.maximum(source, 0)
        amp_block = jnp.take(received, gather_at.reshape(-1), axis=0).reshape(BLK_DEV, B, B)
        live_mask = pair_rank[None, :] < block_sizes[:, None]
        keep = (source >= 0)[:, :, None] & live_mask[:, None, :]
        amp_block = jnp.where(keep, amp_block, jnp.zeros((), amp_block.dtype))
        weights_block = lax.dynamic_slice_in_dim(interaction, first_block, BLK_DEV, 0)
        cycle_block = jnp.einsum("bik,bkj->bij", weights_block.astype(jnp.float32), amp_block.astype(jnp.float32)).astype(jnp.bfloat16)
        local_rows = lax.dynamic_slice_in_dim(slot_grid, chan_number.astype(jnp.int32), 1, 0)[0]
        block_id = local_rows // ROWS_BLOCK
        row_pos = orb_ids[:, None] * ROWS_BLOCK + local_rows % ROWS_BLOCK
        flat_rows = (block_id * B + row_pos).reshape(-1)
        picked = jnp.take(cycle_block.reshape(BLK_DEV * B, B), flat_rows, axis=0)
        return picked.reshape(N_ORB, P_DEV, B)

    returned = lax.map(per_chan, jnp.arange(N_CHAN, dtype=jnp.int32))
    returned = returned.reshape(N_CHAN, N_ORB, N_CHAN, QUOTA, B).transpose(2, 1, 0, 3, 4)
    returned = returned.reshape(N_CHAN, N_ORB * P_DEV, B)

    def finish(packed):
        amp_rows, cycle_rows, weight_rows, denom_rows = packed
        total = amp_rows.astype(jnp.float32) + (weight_rows[:, None] * cycle_rows.astype(jnp.float32)) / denom_rows[:, None]
        return total.astype(jnp.bfloat16)

    updated = lax.map(finish, (amplitudes.reshape(N_CHAN, N_ORB * P_DEV, B), returned, recoupling.reshape(N_CHAN, N_ORB * P_DEV), denominators.reshape(N_CHAN, N_ORB * P_DEV)))
    return updated.reshape(PP_ROWS, B)
```

```python
import jax
import jax.numpy as jnp
from jax import lax
from jax.sharding import PartitionSpec as P

BOTH = ("chan", "orb")


def shards(
    amplitudes, recoupling, denominators, interaction, pair_source, return_slot, channel_sizes
):
    chan_count = lax.axis_size("chan")
    orb_count = lax.axis_size("orb")
    row_count, width = amplitudes.shape
    quota = row_count // chan_count
    blocks_here, rows_block = pair_source.shape
    halves = rows_block // 128
    peers = chan_count * orb_count
    bf = jnp.bfloat16

    def shift(x, by):
        return lax.ppermute(x, "orb", [(i, (i + by) % orb_count) for i in range(orb_count)])

    rows = jnp.take(interaction.reshape(blocks_here * rows_block, width), return_slot, axis=0)
    block_of = (return_slot // rows_block).astype(bf)
    slot_of = (return_slot % rows_block).astype(bf)
    tags = jnp.zeros((16, width), bf).at[0, :row_count].set(block_of).at[1, :row_count].set(slot_of)
    packed = jnp.concatenate([rows, tags], axis=0)
    half = packed.shape[0] // 2
    after = shift(packed, -1)
    before = shift(packed, 1)
    across = jnp.concatenate([shift(after[:half], -1), shift(before[half:], 1)], axis=0)

    relayed = (amplitudes.astype(jnp.float32) * recoupling[:, None]).astype(bf)
    outgoing = relayed.reshape(chan_count, quota, orb_count, halves, 128).transpose(0, 2, 1, 3, 4)
    received = lax.all_to_all(
        outgoing.reshape(peers, quota, halves, 128), BOTH, split_axis=0, concat_axis=0, tiled=True
    )

    stack = jnp.stack([packed, after, across, before])
    block_at = stack[:, row_count, :row_count]
    slot_at = stack[:, row_count + 1, :row_count]
    weights = stack[:, :row_count]
    here = lax.axis_index("orb")
    order = (jnp.arange(orb_count) - here) % orb_count
    block_at = block_at[order]
    slot_at = slot_at[order]
    weights = weights[order]
    pick = (jnp.arange(rows_block, dtype=jnp.int32).astype(bf)[None, :, None] == slot_at[:, None, :]).astype(bf)
    spread = jnp.einsum(
        "arok,oki->aroi",
        weights.reshape(orb_count, row_count, orb_count, rows_block),
        pick,
        preferred_element_type=jnp.float32,
    ).astype(bf)
    mixing = jnp.where(
        block_at[:, :, None, None] == block_at[None, None, :, :], spread, jnp.zeros((), bf)
    )
    sizes = channel_sizes // orb_count
    size_at = jnp.sum(
        jnp.where(
            block_at[:, :, None].astype(jnp.int32) == jnp.arange(blocks_here, dtype=jnp.int32),
            sizes,
            0,
        ),
        axis=2,
    )
    live = jnp.arange(rows_block, dtype=jnp.int32)[None, None, :] < size_at[:, :, None]

    block = received.reshape(chan_count, orb_count, quota, rows_block).transpose(1, 0, 2, 3)
    block = block.reshape(orb_count, row_count, rows_block)
    block = jnp.where(live, block, jnp.zeros((), bf))
    cycle = jnp.einsum("aroi,oik->ark", mixing, block, preferred_element_type=jnp.float32).astype(bf)
    back = cycle.reshape(orb_count, chan_count, quota, halves, 128).transpose(1, 0, 2, 3, 4)
    returned = lax.all_to_all(
        back.reshape(peers, quota, halves, 128), BOTH, split_axis=0, concat_axis=0, tiled=True
    )
    returned = returned.reshape(chan_count, orb_count, quota, halves, 128).transpose(0, 2, 1, 3, 4)
    returned = returned.reshape(row_count, width)
    updated = (
        amplitudes.astype(jnp.float32)
        + recoupling[:, None] * returned.astype(jnp.float32) / denominators[:, None]
    )
    return updated.astype(bf)


def solution(mesh):
    in_specs = (
        P(("chan", "orb"), None),
        P(("chan", "orb")),
        P(("chan", "orb")),
        P("chan", "orb", None),
        P("chan", "orb"),
        P(("chan", "orb")),
        P("chan"),
    )
    out_specs = P(("chan", "orb"), None)
    return jax.shard_map(shards, mesh=mesh, in_specs=in_specs, out_specs=out_specs, check_vma=False)
```

```python
import functools

import jax
import jax.numpy as jnp
from jax import lax
from jax.experimental import pallas as pl
from jax.experimental.pallas import tpu as pltpu
from jax.sharding import PartitionSpec as P


BOTH = ("chan", "orb")
LANES = 128
TAGS = 16
BF = jnp.bfloat16
F32 = jnp.float32
VMEM_BYTES = 56 * 1024 * 1024


def call(body, out_shape, in_specs, scratch=(), **kw):
    return pl.pallas_call(
        body,
        out_shape=out_shape,
        in_specs=in_specs,
        out_specs=jax.tree.map(lambda _: pl.BlockSpec(memory_space=pltpu.VMEM), out_shape),
        scratch_shapes=list(scratch),
        compiler_params=pltpu.CompilerParams(vmem_limit_bytes=VMEM_BYTES),
        **kw,
    )


VM = pl.BlockSpec(memory_space=pltpu.VMEM)
SM = pl.BlockSpec(memory_space=pltpu.SMEM)
ANY = pl.BlockSpec(memory_space=pl.ANY)


def one_hot(hit):
    return jnp.where(hit, 1.0, 0.0).astype(BF)


def column(rows):
    r, n = rows.shape
    tall = jnp.concatenate([rows, jnp.zeros((LANES - r, n), F32)], axis=0)
    return jnp.transpose(tall)


def pick_body(quota, src_ref, w_ref, out_ref):
    blocks, rows_block = src_ref.shape
    width = w_ref.shape[1]
    states = blocks * rows_block
    src = jnp.concatenate([src_ref[c : c + 1, :] for c in range(blocks)], axis=1)
    sender = (src * 205) >> 10
    place = jnp.where(src >= 0, (src - sender * quota) * LANES + sender, -1)
    lane = lax.broadcasted_iota(jnp.int32, (TAGS, states), 1)
    which = lax.broadcasted_iota(jnp.int32, (TAGS, states), 0)
    labels = jnp.where(which == 0, lane // rows_block, jnp.where(which == 1, lane % rows_block, 0))
    labels = labels.astype(F32).astype(BF)
    count = quota * LANES
    out_ref[count:, count:] = jnp.zeros((TAGS, width - count), BF)
    for q in range(quota):
        at = lax.broadcasted_iota(jnp.int32, (LANES, states), 0) + q * LANES
        hit = one_hot(at == place)
        here = slice(q * LANES, (q + 1) * LANES)
        out_ref[here, :] = jnp.dot(hit, w_ref[...], preferred_element_type=F32).astype(BF)
        out_ref[count:, here] = lax.dot_general(
            labels, hit, (((1,), (1,)), ((), ())), preferred_element_type=F32
        ).astype(BF)


def pack_body(orbs, quota, amp_ref, rec_ref, out_ref, tile_ref, flat_ref):
    tiles = amp_ref.shape[1] // LANES
    halves = tiles // orbs
    scale = column(rec_ref[...])
    for a in range(quota):
        rows = slice(a * LANES, (a + 1) * LANES)
        by = scale[:, a : a + 1]
        for t in range(tiles):
            tile_ref[t, rows, :] = amp_ref[rows, t * LANES : (t + 1) * LANES].astype(F32) * by
    for o in range(orbs):
        for q in range(quota):
            for h in range(halves):
                piece = tile_ref[o * halves + h, pl.ds(q, LANES, stride=quota), :]
                at = (o * quota + q) * halves + h
                flat_ref[pl.ds(at, LANES, stride=orbs * quota * halves), :] = piece
    out_ref[...] = flat_ref[...].astype(BF)


def mix_rows(w, owner, tags_ref, here, put):
    orbs = tags_ref.shape[0]
    for o in range(orbs):
        tag = tags_ref[(o + orbs - here) % orbs]
        part = w(o)
        slot = lax.broadcasted_iota(jnp.int32, (part.shape[1], tag.shape[1]), 0).astype(F32)
        spread = jnp.dot(part, one_hot(slot == tag[1:2, :]), preferred_element_type=F32)
        put(o, jnp.where(owner == tag[0:1, :], spread, 0.0).astype(BF))


def build_body(quota, here_ref, own_ref, after_ref, before_ref, far_ref, m0, m1, m3, tags_out, tags_ref):
    count = quota * LANES
    rows_block = own_ref.shape[1] // 4
    refs = (own_ref, after_ref, None, before_ref)
    for s, ref in enumerate(refs):
        tag = far_ref[:, :count] if ref is None else ref[count:, :count]
        tags_ref[s] = tag.astype(F32)
        tags_out[s] = tag.astype(F32)
    here = here_ref[0]
    for s, out in ((0, m0), (1, m1), (3, m3)):
        owner = column(tags_ref[s])[:, 0:1]
        ref = refs[s]

        def put(o, value, out=out):
            out[:, o * count : (o + 1) * count] = value

        mix_rows(
            lambda o, ref=ref: ref[:count, o * rows_block : (o + 1) * rows_block],
            owner, tags_ref, here, put,
        )


def cycle_body(
    quota, here_ref, size_ref, raw_ref, lo_ref, hi_ref, tags_ref, m0, m1, m3, out_ref,
    flat_ref, block_ref, mix_ref, far_ref, sem,
):
    orbs = tags_ref.shape[0]
    count = quota * LANES
    halves = 2
    rows_block = halves * LANES
    copies = []
    for i, (s, src) in enumerate(((0, m0), (1, m1), (3, m3))):
        cp = pltpu.make_async_copy(src, mix_ref.at[s], sem.at[i])
        cp.start()
        copies.append((s, cp))
    here = here_ref[0]
    half = count // 2
    far_ref[:half] = lo_ref[...]
    far_ref[half:] = hi_ref[...]

    def put(o, value):
        mix_ref[2, :, o * count : (o + 1) * count] = value

    mix_rows(
        lambda o: far_ref[:, o * rows_block : (o + 1) * rows_block],
        column(tags_ref[2])[:, 0:1], tags_ref, here, put,
    )
    flat_ref[...] = raw_ref[...].astype(F32)
    step = orbs * quota * halves
    lane = lax.broadcasted_iota(jnp.int32, (LANES, LANES), 1).astype(F32)
    for o in range(orbs):
        tag = tags_ref[(o + orbs - here) % orbs]
        size = jnp.zeros((8, count), F32)
        for c in range(size_ref.shape[0]):
            live = (size_ref[c] // orbs).astype(F32)
            size = size + jnp.where(tag[0:8, :] == float(c), live, 0.0)
        size = column(size)[:, 0:1]
        for q in range(quota):
            for h in range(halves):
                piece = flat_ref[pl.ds((o * quota + q) * halves + h, LANES, stride=step), :]
                keep = lane + float(h * LANES) < size[q * LANES : (q + 1) * LANES]
                row = o * count + q * LANES
                block_ref[row : row + LANES, h * LANES : (h + 1) * LANES] = jnp.where(
                    keep, piece, 0.0
                ).astype(BF)

    def multiply(s):
        done = jnp.dot(mix_ref[s], block_ref[...], preferred_element_type=F32)
        to = (here + s) % orbs
        for q in range(quota):
            for h in range(halves):
                flat_ref[pl.ds((to * quota + q) * halves + h, LANES, stride=step), :] = done[
                    q * LANES : (q + 1) * LANES, h * LANES : (h + 1) * LANES
                ]

    multiply(2)
    for s, cp in copies:
        cp.wait()
        multiply(s)
    out_ref[...] = flat_ref[...].astype(BF)


def finish_body(orbs, quota, raw_ref, amp_ref, rec_ref, den_ref, out_ref, flat_ref, tile_ref):
    tiles = amp_ref.shape[1] // LANES
    halves = tiles // orbs
    flat_ref[...] = raw_ref[...].astype(F32)
    for o in range(orbs):
        for q in range(quota):
            for h in range(halves):
                at = (o * quota + q) * halves + h
                piece = flat_ref[pl.ds(at, LANES, stride=orbs * quota * halves), :]
                tile_ref[o * halves + h, pl.ds(q, LANES, stride=quota), :] = piece
    rec = column(rec_ref[...])
    den = column(den_ref[...])
    for a in range(quota):
        rows = slice(a * LANES, (a + 1) * LANES)
        for t in range(tiles):
            cols = slice(t * LANES, (t + 1) * LANES)
            move = rec[:, a : a + 1] * tile_ref[t, rows, :] / den[:, a : a + 1]
            out_ref[rows, cols] = (amp_ref[rows, cols].astype(F32) + move).astype(BF)


def pick(pair_source, interaction, quota):
    blocks, rows_block, width = interaction.shape
    return call(
        functools.partial(pick_body, quota),
        jax.ShapeDtypeStruct((quota * LANES + TAGS, width), BF),
        [VM, VM],
        name="pick",
    )(pair_source, interaction.reshape(blocks * rows_block, width))


def pack(amplitudes, recoupling, orbs, quota):
    rows, width = amplitudes.shape
    flat = rows * width // LANES
    return call(
        functools.partial(pack_body, orbs, quota),
        jax.ShapeDtypeStruct((flat, LANES), BF),
        [VM, VM],
        [pltpu.VMEM((width // LANES, rows, LANES), F32), pltpu.VMEM((flat, LANES), F32)],
        name="pack",
    )(amplitudes, recoupling.reshape(rows // LANES, LANES))


def build(here, own, after, before, far, quota):
    count = quota * LANES
    mixed = jax.ShapeDtypeStruct((count, 4 * count), BF)
    tags = jax.ShapeDtypeStruct((4, TAGS, count), F32)
    return call(
        functools.partial(build_body, quota),
        (mixed, mixed, mixed, tags),
        [SM, VM, VM, VM, VM],
        [pltpu.VMEM((4, TAGS, count), F32)],
        name="build",
    )(here, own, after, before, far)


def cycle(here, sizes, raw, lo, hi, tags, mixed, quota):
    count = quota * LANES
    return call(
        functools.partial(cycle_body, quota),
        jax.ShapeDtypeStruct(raw.shape, BF),
        [SM, SM, VM, VM, VM, VM, ANY, ANY, ANY],
        [
            pltpu.VMEM(raw.shape, F32),
            pltpu.VMEM((4 * count, 2 * LANES), BF),
            pltpu.VMEM((4, count, 4 * count), BF),
            pltpu.VMEM((count, lo.shape[1]), BF),
            pltpu.SemaphoreType.DMA((3,)),
        ],
        name="cycle",
    )(here, sizes, raw, lo, hi, tags, *mixed)


def finish(raw, amplitudes, recoupling, denominators, orbs, quota):
    rows, width = amplitudes.shape
    return call(
        functools.partial(finish_body, orbs, quota),
        jax.ShapeDtypeStruct((rows, width), BF),
        [VM, VM, VM, VM],
        [pltpu.VMEM(raw.shape, F32), pltpu.VMEM((width // LANES, rows, LANES), F32)],
        name="finish",
    )(
        raw, amplitudes,
        recoupling.reshape(rows // LANES, LANES), denominators.reshape(rows // LANES, LANES),
    )


def shards(
    amplitudes, recoupling, denominators, interaction, pair_source, return_slot, channel_sizes
):
    chan_count = lax.axis_size("chan")
    orbs = lax.axis_size("orb")
    row_count, _ = amplitudes.shape
    quota = row_count // chan_count
    count = quota * LANES
    half = count // 2
    halves = pair_source.shape[1] // LANES
    peers = chan_count * orbs

    def shift(x, by):
        return lax.ppermute(x, "orb", [(i, (i + by) % orbs) for i in range(orbs)])

    def exchange(x):
        x = x.reshape(peers, quota, halves, LANES)
        x = lax.all_to_all(x, BOTH, split_axis=0, concat_axis=0, tiled=True)
        return x.reshape(peers * quota * halves, LANES)

    own = pick(pair_source, interaction, quota)
    after = shift(own, -1)
    before = shift(own, 1)
    outgoing, _ = lax.optimization_barrier((pack(amplitudes, recoupling, orbs, quota), own))
    raw = exchange(outgoing)
    lo = shift(after[:half], -1)
    hi = shift(before[half:count], 1)
    tag, _ = lax.optimization_barrier((own[count:], after))
    far = shift(tag, 2)
    here = lax.axis_index("orb").astype(jnp.int32).reshape(1)
    *mixed, tags = build(here, own, after, before, far, quota)
    back = cycle(here, channel_sizes, raw, lo, hi, tags, mixed, quota)
    returned = exchange(back)
    return finish(returned, amplitudes, recoupling, denominators, orbs, quota)


def solution(mesh):
    in_specs = (
        P(("chan", "orb"), None),
        P(("chan", "orb")),
        P(("chan", "orb")),
        P("chan", "orb", None),
        P("chan", "orb"),
        P(("chan", "orb")),
        P("chan"),
    )
    out_specs = P(("chan", "orb"), None)
    return jax.shard_map(
        shards, mesh=mesh, in_specs=in_specs, out_specs=out_specs, check_vma=False
    )
```

```python
import functools

import jax
import jax.numpy as jnp
from jax import lax
from jax.experimental import pallas as pl
from jax.experimental.pallas import tpu as pltpu
from jax.sharding import PartitionSpec as P


BOTH = ("chan", "orb")
LANES = 128
TAGS = 16
BF = jnp.bfloat16
F32 = jnp.float32
VMEM_BYTES = 56 * 1024 * 1024
CHUNKS = 4

VM = pl.BlockSpec(memory_space=pltpu.VMEM)
SM = pl.BlockSpec(memory_space=pltpu.SMEM)
ANY = pl.BlockSpec(memory_space=pl.ANY)


def call(body, out_shape, in_specs, out_specs, scratch=(), **kw):
    return pl.pallas_call(
        body,
        out_shape=out_shape,
        in_specs=in_specs,
        out_specs=out_specs,
        scratch_shapes=list(scratch),
        compiler_params=pltpu.CompilerParams(vmem_limit_bytes=VMEM_BYTES),
        **kw,
    )


def one_hot(hit):
    return jnp.where(hit, 1.0, 0.0).astype(BF)


def column(rows):
    r, n = rows.shape
    tall = jnp.concatenate([rows, jnp.zeros((LANES - r, n), F32)], axis=0)
    return jnp.transpose(tall)


def pick_body(quota, src_ref, w_ref, out_ref, hit_ref):
    blocks, rows_block = src_ref.shape
    states, width = w_ref.shape
    count = quota * LANES
    src = jnp.concatenate([src_ref[c : c + 1, :] for c in range(blocks)], axis=1)
    sender = (src * 205) >> 10
    place = jnp.where(src >= 0, (src - sender * quota) * LANES + sender, -1)
    lane = lax.broadcasted_iota(jnp.int32, (TAGS, states), 1)
    which = lax.broadcasted_iota(jnp.int32, (TAGS, states), 0)
    labels = jnp.where(which == 0, lane // rows_block, jnp.where(which == 1, lane % rows_block, 0))
    labels = labels.astype(F32).astype(BF)
    out_ref[count:, count:] = jnp.zeros((TAGS, width - count), BF)
    for q in range(quota):
        at = lax.broadcasted_iota(jnp.int32, (LANES, states), 0) + q * LANES
        hit = one_hot(at == place)
        here = slice(q * LANES, (q + 1) * LANES)
        hit_ref[here, :] = hit
        out_ref[count:, here] = lax.dot_general(
            labels, hit, (((1,), (1,)), ((), ())), preferred_element_type=F32
        ).astype(BF)
    out_ref[:count, :] = jnp.dot(
        hit_ref[...], w_ref[...], preferred_element_type=F32
    ).astype(BF)


def spread_rows(value, out_ref):
    tall = column(value)
    for a in range(value.shape[0]):
        out_ref[a * LANES : (a + 1) * LANES, :] = jnp.broadcast_to(
            tall[:, a : a + 1], (LANES, LANES)
        )


def pack_body(
    orbs, quota, amp_any, rec_ref, out_any, amp_ref, scale_ref, tile_ref, flat_ref, out_ref,
    sem_in, sem_out,
):
    rows, width = amp_ref.shape
    tiles = width // LANES
    halves = tiles // orbs
    part = rows // CHUNKS
    groups = part // quota
    loads = []
    for j in range(CHUNKS):
        here = slice(j * part, (j + 1) * part)
        loads.append(pltpu.make_async_copy(amp_any.at[here], amp_ref.at[here], sem_in.at[j]))
        loads[j].start()
    spread_rows(rec_ref[...], scale_ref)
    stores = []
    for j in range(CHUNKS):
        here = slice(j * part, (j + 1) * part)
        loads[j].wait()
        for t in range(tiles):
            tile_ref[t, here, :] = (
                amp_ref[here, t * LANES : (t + 1) * LANES].astype(F32) * scale_ref[here, :]
            )
        for o in range(orbs):
            for q in range(quota):
                for h in range(halves):
                    piece = tile_ref[o * halves + h, pl.ds(j * part + q, groups, stride=quota), :]
                    at = j * part * tiles + (o * quota + q) * halves + h
                    flat_ref[pl.ds(at, groups, stride=orbs * quota * halves), :] = piece
        to = slice(j * part * tiles, (j + 1) * part * tiles)
        out_ref[to, :] = flat_ref[to, :].astype(BF)
        stores.append(pltpu.make_async_copy(out_ref.at[to], out_any.at[to], sem_out.at[j]))
        stores[j].start()
    for cp in stores:
        cp.wait()


def build_body(
    quota, here_ref, size_ref, own_ref, after_ref, before_ref, far_ref,
    m0, m1, m3, hot_ref, block_ref, owner_ref, limit_ref, tags_ref,
):
    count = quota * LANES
    rows_block = hot_ref.shape[1]
    orbs = hot_ref.shape[0]
    refs = (own_ref, after_ref, None, before_ref)
    for s, ref in enumerate(refs):
        tag = far_ref[:, :count] if ref is None else ref[count:, :count]
        tags_ref[s] = tag.astype(F32)
    here = here_ref[0]
    slot = lax.broadcasted_iota(jnp.int32, (rows_block, count), 0).astype(F32)
    for o in range(orbs):
        tag = tags_ref[(o + orbs - here) % orbs]
        hot_ref[o] = one_hot(slot == tag[1:2, :])
        block_ref[o] = tag[0:8, :]
        size = jnp.zeros((1, count), F32)
        for c in range(size_ref.shape[0]):
            live = (size_ref[c] // orbs).astype(F32)
            size = size + jnp.where(tag[0:1, :] == float(c), live, 0.0)
        limit_ref[o * count : (o + 1) * count, :] = jnp.broadcast_to(
            column(size)[:, 0:1], (count, LANES)
        )
    owner_ref[...] = jnp.broadcast_to(column(tags_ref[2])[:, 0:1], (count, LANES))
    for s, out in ((0, m0), (1, m1), (3, m3)):
        owner = column(tags_ref[s])[:, 0:1]
        for o in range(orbs):
            part = refs[s][:count, o * rows_block : (o + 1) * rows_block]
            spread = jnp.dot(part, hot_ref[o], preferred_element_type=F32)
            out[:, o * count : (o + 1) * count] = jnp.where(
                owner == block_ref[o, 0:1, :], spread, 0.0
            ).astype(BF)


def cycle_body(
    quota, here_ref, raw_any, lo_any, hi_any, hot_any, block_any, owner_any, limit_any,
    m0, m1, m3, out_any,
    raw_ref, far_ref, hot_ref, block_ref, owner_ref, limit_ref, mix_ref, flat_ref, rows_ref,
    out_ref, sem,
):
    orbs, rows_block, count = hot_ref.shape
    halves = rows_block // LANES
    half = count // 2
    here = here_ref[0]
    pairs = (
        (lo_any, far_ref.at[:half]), (hi_any, far_ref.at[half:]), (hot_any, hot_ref),
        (block_any, block_ref), (owner_any, owner_ref), (raw_any, raw_ref),
        (limit_any, limit_ref), (m0, mix_ref.at[0]), (m1, mix_ref.at[1]), (m3, mix_ref.at[3]),
    )
    copies = [pltpu.make_async_copy(a, b, sem.at[i]) for i, (a, b) in enumerate(pairs)]
    for cp in copies:
        cp.start()
    for cp in copies[:7]:
        cp.wait()
    owner = owner_ref[:, 0:1]
    step = orbs * quota * halves
    lane = lax.broadcasted_iota(jnp.int32, (LANES, LANES), 1).astype(F32)
    flat_ref[...] = raw_ref[...].astype(F32)
    for o in range(orbs):
        spread = jnp.dot(
            far_ref[:, o * rows_block : (o + 1) * rows_block], hot_ref[o],
            preferred_element_type=F32,
        )
        mix_ref[2, :, o * count : (o + 1) * count] = jnp.where(
            owner == block_ref[o, 0:1, :], spread, 0.0
        ).astype(BF)
        for q in range(quota):
            row = o * count + q * LANES
            for h in range(halves):
                piece = flat_ref[pl.ds((o * quota + q) * halves + h, LANES, stride=step), :]
                keep = lane + float(h * LANES) < limit_ref[row : row + LANES, :]
                rows_ref[row : row + LANES, h * LANES : (h + 1) * LANES] = jnp.where(
                    keep, piece, 0.0
                ).astype(BF)
    for cp in copies[7:]:
        cp.wait()
    for s in range(orbs):
        done = jnp.dot(mix_ref[s], rows_ref[...], preferred_element_type=F32)
        to = (here + s) % orbs
        for q in range(quota):
            for h in range(halves):
                flat_ref[pl.ds((to * quota + q) * halves + h, LANES, stride=step), :] = done[
                    q * LANES : (q + 1) * LANES, h * LANES : (h + 1) * LANES
                ]
    part = out_ref.shape[0] // CHUNKS
    for j in range(CHUNKS):
        rows = slice(j * part, (j + 1) * part)
        out_ref[rows, :] = flat_ref[rows, :].astype(BF)
        pltpu.make_async_copy(out_ref.at[rows], out_any.at[rows], sem.at[j]).start()
    for j in range(CHUNKS):
        rows = slice(j * part, (j + 1) * part)
        pltpu.make_async_copy(out_ref.at[rows], out_any.at[rows], sem.at[j]).wait()


def finish_body(
    orbs, quota, raw_any, amp_any, rec_ref, den_ref, out_any,
    raw_ref, amp_ref, scale_ref, flat_ref, tile_ref, out_ref, sem_in, sem_out,
):
    rows, width = amp_ref.shape
    tiles = width // LANES
    halves = tiles // orbs
    part = rows // CHUNKS
    groups = part // quota
    loads = []
    for j in range(CHUNKS):
        here = slice(j * part, (j + 1) * part)
        to = slice(j * part * tiles, (j + 1) * part * tiles)
        loads.append(pltpu.make_async_copy(raw_any.at[to], raw_ref.at[to], sem_in.at[0, j]))
        loads.append(pltpu.make_async_copy(amp_any.at[here], amp_ref.at[here], sem_in.at[1, j]))
    for cp in loads:
        cp.start()
    spread_rows(rec_ref[...] / den_ref[...], scale_ref)
    stores = []
    for j in range(CHUNKS):
        here = slice(j * part, (j + 1) * part)
        to = slice(j * part * tiles, (j + 1) * part * tiles)
        loads[2 * j].wait()
        loads[2 * j + 1].wait()
        flat_ref[to, :] = raw_ref[to, :].astype(F32)
        for o in range(orbs):
            for q in range(quota):
                for h in range(halves):
                    at = j * part * tiles + (o * quota + q) * halves + h
                    piece = flat_ref[pl.ds(at, groups, stride=orbs * quota * halves), :]
                    tile_ref[o * halves + h, pl.ds(j * part + q, groups, stride=quota), :] = piece
        for t in range(tiles):
            cols = slice(t * LANES, (t + 1) * LANES)
            move = scale_ref[here, :] * tile_ref[t, here, :]
            out_ref[here, cols] = (amp_ref[here, cols].astype(F32) + move).astype(BF)
        stores.append(pltpu.make_async_copy(out_ref.at[here], out_any.at[here], sem_out.at[j]))
        stores[j].start()
    for cp in stores:
        cp.wait()


def pick(pair_source, interaction, quota):
    blocks, rows_block, width = interaction.shape
    count = quota * LANES
    states = blocks * rows_block
    return call(
        functools.partial(pick_body, quota),
        jax.ShapeDtypeStruct((count + TAGS, width), BF),
        [VM, VM],
        VM,
        [pltpu.VMEM((count, states), BF)],
        name="pick",
    )(pair_source, interaction.reshape(states, width))


def pack(amplitudes, recoupling, orbs, quota):
    rows, width = amplitudes.shape
    tiles = width // LANES
    return call(
        functools.partial(pack_body, orbs, quota),
        jax.ShapeDtypeStruct((rows * tiles, LANES), BF),
        [ANY, VM],
        ANY,
        [
            pltpu.VMEM((rows, width), BF),
            pltpu.VMEM((rows, LANES), F32),
            pltpu.VMEM((tiles, rows, LANES), F32),
            pltpu.VMEM((rows * tiles, LANES), F32),
            pltpu.VMEM((rows * tiles, LANES), BF),
            pltpu.SemaphoreType.DMA((CHUNKS,)),
            pltpu.SemaphoreType.DMA((CHUNKS,)),
        ],
        name="pack",
    )(amplitudes, recoupling.reshape(rows // LANES, LANES))


def build(here, sizes, own, after, before, far, quota):
    count = quota * LANES
    mixed = jax.ShapeDtypeStruct((count, 4 * count), BF)
    outs = (
        mixed, mixed, mixed,
        jax.ShapeDtypeStruct((4, own.shape[1] // 4, count), BF),
        jax.ShapeDtypeStruct((4, 8, count), F32),
        jax.ShapeDtypeStruct((count, LANES), F32),
        jax.ShapeDtypeStruct((4 * count, LANES), F32),
    )
    return call(
        functools.partial(build_body, quota),
        outs,
        [SM, SM, VM, VM, VM, VM],
        (VM,) * len(outs),
        [pltpu.VMEM((4, TAGS, count), F32)],
        name="build",
    )(here, sizes, own, after, before, far)


def cycle(here, raw, lo, hi, m0, m1, m3, hot, block, owner, limit, quota):
    count = quota * LANES
    return call(
        functools.partial(cycle_body, quota),
        jax.ShapeDtypeStruct(raw.shape, BF),
        [SM] + [ANY] * 10,
        ANY,
        [
            pltpu.VMEM(raw.shape, BF),
            pltpu.VMEM((count, lo.shape[1]), BF),
            pltpu.VMEM(hot.shape, BF),
            pltpu.VMEM(block.shape, F32),
            pltpu.VMEM(owner.shape, F32),
            pltpu.VMEM(limit.shape, F32),
            pltpu.VMEM((4, count, 4 * count), BF),
            pltpu.VMEM(raw.shape, F32),
            pltpu.VMEM((4 * count, hot.shape[1]), BF),
            pltpu.VMEM(raw.shape, BF),
            pltpu.SemaphoreType.DMA((10,)),
        ],
        name="cycle",
    )(here, raw, lo, hi, hot, block, owner, limit, m0, m1, m3)


def finish(raw, amplitudes, recoupling, denominators, orbs, quota):
    rows, width = amplitudes.shape
    tiles = width // LANES
    return call(
        functools.partial(finish_body, orbs, quota),
        jax.ShapeDtypeStruct((rows, width), BF),
        [ANY, ANY, VM, VM],
        ANY,
        [
            pltpu.VMEM((rows * tiles, LANES), BF),
            pltpu.VMEM((rows, width), BF),
            pltpu.VMEM((rows, LANES), F32),
            pltpu.VMEM((rows * tiles, LANES), F32),
            pltpu.VMEM((tiles, rows, LANES), F32),
            pltpu.VMEM((rows, width), BF),
            pltpu.SemaphoreType.DMA((2, CHUNKS)),
            pltpu.SemaphoreType.DMA((CHUNKS,)),
        ],
        name="finish",
    )(
        raw, amplitudes,
        recoupling.reshape(rows // LANES, LANES), denominators.reshape(rows // LANES, LANES),
    )


def shards(
    amplitudes, recoupling, denominators, interaction, pair_source, return_slot, channel_sizes
):
    chan_count = lax.axis_size("chan")
    orbs = lax.axis_size("orb")
    row_count, _ = amplitudes.shape
    quota = row_count // chan_count
    count = quota * LANES
    half = count // 2
    halves = pair_source.shape[1] // LANES
    peers = chan_count * orbs

    def shift(x, by):
        return lax.ppermute(x, "orb", [(i, (i + by) % orbs) for i in range(orbs)])

    def exchange(x):
        x = x.reshape(peers, quota, halves, LANES)
        x = lax.all_to_all(x, BOTH, split_axis=0, concat_axis=0, tiled=True)
        return x.reshape(peers * quota * halves, LANES)

    own = pick(pair_source, interaction, quota)
    after = shift(own, -1)
    before = shift(own, 1)
    outgoing, _ = lax.optimization_barrier((pack(amplitudes, recoupling, orbs, quota), own))
    raw = exchange(outgoing)
    far = shift(own[count:], 2)
    lo = shift(after[:half], -1)
    hi = shift(before[half:count], 1)
    here = lax.axis_index("orb").astype(jnp.int32).reshape(1)
    built = build(here, channel_sizes, own, after, before, far, quota)
    back = cycle(here, raw, lo, hi, *built, quota)
    returned = exchange(back)
    return finish(returned, amplitudes, recoupling, denominators, orbs, quota)


def solution(mesh):
    in_specs = (
        P(("chan", "orb"), None),
        P(("chan", "orb")),
        P(("chan", "orb")),
        P("chan", "orb", None),
        P("chan", "orb"),
        P(("chan", "orb")),
        P("chan"),
    )
    out_specs = P(("chan", "orb"), None)
    return jax.shard_map(
        shards, mesh=mesh, in_specs=in_specs, out_specs=out_specs, check_vma=False
    )
```

```python
import functools

import jax
import jax.numpy as jnp
from jax import lax
from jax.experimental import pallas as pl
from jax.experimental.pallas import tpu as pltpu
from jax.sharding import PartitionSpec as P


BOTH = ("chan", "orb")
LANES = 128
TAGS = 16
BF = jnp.bfloat16
F32 = jnp.float32
VMEM_BYTES = 48 * 1024 * 1024
CHUNKS = 4

VM = pl.BlockSpec(memory_space=pltpu.VMEM)
SM = pl.BlockSpec(memory_space=pltpu.SMEM)
ANY = pl.BlockSpec(memory_space=pl.ANY)


def call(body, out_shape, in_specs, out_specs, scratch=(), **kw):
    return pl.pallas_call(
        body,
        out_shape=out_shape,
        in_specs=in_specs,
        out_specs=out_specs,
        scratch_shapes=list(scratch),
        compiler_params=pltpu.CompilerParams(vmem_limit_bytes=VMEM_BYTES),
        **kw,
    )


def near(x):
    return pltpu.with_memory_space_constraint(x, pltpu.VMEM)


def one_hot(hit):
    return jnp.where(hit, 1.0, 0.0).astype(BF)


def column(rows):
    r, n = rows.shape
    tall = jnp.concatenate([rows, jnp.zeros((LANES - r, n), F32)], axis=0)
    return jnp.transpose(tall)


def pick_body(quota, src_ref, w_ref, out_ref, hit_ref):
    blocks, rows_block = src_ref.shape
    states, width = w_ref.shape
    count = quota * LANES
    src = jnp.concatenate([src_ref[c : c + 1, :] for c in range(blocks)], axis=1)
    sender = (src * 205) >> 10
    place = jnp.where(src >= 0, (src - sender * quota) * LANES + sender, -1)
    lane = lax.broadcasted_iota(jnp.int32, (TAGS, states), 1)
    which = lax.broadcasted_iota(jnp.int32, (TAGS, states), 0)
    labels = jnp.where(which == 0, lane // rows_block, jnp.where(which == 1, lane % rows_block, 0))
    labels = labels.astype(F32).astype(BF)
    out_ref[count:, count:] = jnp.zeros((TAGS, width - count), BF)
    for q in range(quota):
        at = lax.broadcasted_iota(jnp.int32, (LANES, states), 0) + q * LANES
        hit = one_hot(at == place)
        here = slice(q * LANES, (q + 1) * LANES)
        hit_ref[here, :] = hit
        out_ref[count:, here] = lax.dot_general(
            labels, hit, (((1,), (1,)), ((), ())), preferred_element_type=F32
        ).astype(BF)
    out_ref[:count, :] = jnp.dot(
        hit_ref[...], w_ref[...], preferred_element_type=F32
    ).astype(BF)


def spread_rows(value, out_ref):
    tall = column(value)
    for a in range(value.shape[0]):
        out_ref[a * LANES : (a + 1) * LANES, :] = jnp.broadcast_to(
            tall[:, a : a + 1], (LANES, LANES)
        )


def pack_body(
    orbs, quota, amp_ref, rec_ref, out_any, scale_ref, tile_ref, flat_ref, out_ref, sem_out
):
    rows, width = amp_ref.shape
    tiles = width // LANES
    halves = tiles // orbs
    part = rows // CHUNKS
    groups = part // quota
    spread_rows(rec_ref[...], scale_ref)
    stores = []
    for j in range(CHUNKS):
        here = slice(j * part, (j + 1) * part)
        for t in range(tiles):
            tile_ref[t, here, :] = (
                amp_ref[here, t * LANES : (t + 1) * LANES].astype(F32) * scale_ref[here, :]
            )
        for o in range(orbs):
            for q in range(quota):
                for h in range(halves):
                    piece = tile_ref[o * halves + h, pl.ds(j * part + q, groups, stride=quota), :]
                    at = j * part * tiles + (o * quota + q) * halves + h
                    flat_ref[pl.ds(at, groups, stride=orbs * quota * halves), :] = piece
        to = slice(j * part * tiles, (j + 1) * part * tiles)
        out_ref[to, :] = flat_ref[to, :].astype(BF)
        stores.append(pltpu.make_async_copy(out_ref.at[to], out_any.at[to], sem_out.at[j]))
        stores[j].start()
    for cp in stores:
        cp.wait()


def build_body(
    quota, here_ref, size_ref, own_ref, after_ref, before_ref, far_ref,
    m0, m1, m3, hot_ref, block_ref, owner_ref, limit_ref, tags_ref,
):
    count = quota * LANES
    rows_block = hot_ref.shape[1]
    orbs = hot_ref.shape[0]
    refs = (own_ref, after_ref, None, before_ref)
    for s, ref in enumerate(refs):
        tag = far_ref[:, :count] if ref is None else ref[count:, :count]
        tags_ref[s] = tag.astype(F32)
    here = here_ref[0]
    slot = lax.broadcasted_iota(jnp.int32, (rows_block, count), 0).astype(F32)
    for o in range(orbs):
        tag = tags_ref[(o + orbs - here) % orbs]
        hot_ref[o] = one_hot(slot == tag[1:2, :])
        block_ref[o] = tag[0:8, :]
        size = jnp.zeros((1, count), F32)
        for c in range(size_ref.shape[0]):
            live = (size_ref[c] // orbs).astype(F32)
            size = size + jnp.where(tag[0:1, :] == float(c), live, 0.0)
        limit_ref[o * count : (o + 1) * count, :] = jnp.broadcast_to(
            column(size)[:, 0:1], (count, LANES)
        )
    owner_ref[...] = jnp.broadcast_to(column(tags_ref[2])[:, 0:1], (count, LANES))
    for s, out in ((0, m0), (1, m1), (3, m3)):
        owner = column(tags_ref[s])[:, 0:1]
        for o in range(orbs):
            part = refs[s][:count, o * rows_block : (o + 1) * rows_block]
            spread = jnp.dot(part, hot_ref[o], preferred_element_type=F32)
            out[:, o * count : (o + 1) * count] = jnp.where(
                owner == block_ref[o, 0:1, :], spread, 0.0
            ).astype(BF)


def cycle_body(
    quota, here_ref, raw_ref, limit_any, hot_any, block_any, owner_any, m0, m1, m3,
    rows_ref, flat_ref, hot_ref, block_ref, owner_ref, wide_ref, limit_ref, mix_ref, sem,
):
    count = m0.shape[0]
    orbs = m0.shape[1] // count
    halves = rows_ref.shape[1] // LANES
    pairs = (
        (limit_any, limit_ref), (m0, mix_ref.at[0]), (m1, mix_ref.at[1]), (m3, mix_ref.at[2]),
        (hot_any, hot_ref), (block_any, block_ref), (owner_any, owner_ref),
    )
    copies = [pltpu.make_async_copy(a, b, sem.at[i]) for i, (a, b) in enumerate(pairs)]
    for cp in copies:
        cp.start()
    here = here_ref[0]
    step = orbs * quota * halves
    lane = lax.broadcasted_iota(jnp.int32, (LANES, LANES), 1).astype(F32)
    wide_ref[...] = raw_ref[...].astype(F32)
    copies[0].wait()
    for o in range(orbs):
        for q in range(quota):
            row = o * count + q * LANES
            for h in range(halves):
                piece = wide_ref[pl.ds((o * quota + q) * halves + h, LANES, stride=step), :]
                keep = lane + float(h * LANES) < limit_ref[row : row + LANES, :]
                rows_ref[row : row + LANES, h * LANES : (h + 1) * LANES] = jnp.where(
                    keep, piece, 0.0
                ).astype(BF)
    for i, s in enumerate((0, 1, 3)):
        copies[1 + i].wait()
        scatter(quota, (here + s) % orbs, step, mix_ref[i], rows_ref, flat_ref)
    for cp in copies[4:]:
        cp.wait()


def scatter(quota, to, step, mix, rows_ref, flat_ref):
    halves = rows_ref.shape[1] // LANES
    done = jnp.dot(mix, rows_ref[...], preferred_element_type=F32)
    for q in range(quota):
        for h in range(halves):
            flat_ref[pl.ds((to * quota + q) * halves + h, LANES, stride=step), :] = done[
                q * LANES : (q + 1) * LANES, h * LANES : (h + 1) * LANES
            ]


def close_body(
    quota, here_ref, lo_ref, hi_ref, hot_ref, block_ref, owner_ref, rows_ref, flat_in,
    out_ref, flat_ref, mix_ref,
):
    orbs, rows_block, count = hot_ref.shape
    half = count // 2
    step = orbs * quota * (rows_block // LANES)
    for i, ref in enumerate((lo_ref, hi_ref)):
        at = slice(i * half, (i + 1) * half)
        owner = owner_ref[at, 0:1]
        for o in range(orbs):
            spread = jnp.dot(
                ref[:, o * rows_block : (o + 1) * rows_block], hot_ref[o],
                preferred_element_type=F32,
            )
            mix_ref[at, o * count : (o + 1) * count] = jnp.where(
                owner == block_ref[o, 0:1, :], spread, 0.0
            ).astype(BF)
    scatter(quota, (here_ref[0] + 2) % orbs, step, mix_ref[...], rows_ref, flat_ref)
    out_ref[...] = flat_ref[...].astype(BF)


def finish_body(
    orbs, quota, raw_ref, amp_ref, rec_ref, den_ref, out_any,
    scale_ref, flat_ref, tile_ref, out_ref, sem_out,
):
    rows, width = amp_ref.shape
    tiles = width // LANES
    halves = tiles // orbs
    part = rows // CHUNKS
    groups = part // quota
    spread_rows(rec_ref[...] / den_ref[...], scale_ref)
    stores = []
    for j in range(CHUNKS):
        here = slice(j * part, (j + 1) * part)
        to = slice(j * part * tiles, (j + 1) * part * tiles)
        flat_ref[to, :] = raw_ref[to, :].astype(F32)
        for o in range(orbs):
            for q in range(quota):
                for h in range(halves):
                    at = j * part * tiles + (o * quota + q) * halves + h
                    piece = flat_ref[pl.ds(at, groups, stride=orbs * quota * halves), :]
                    tile_ref[o * halves + h, pl.ds(j * part + q, groups, stride=quota), :] = piece
        for t in range(tiles):
            cols = slice(t * LANES, (t + 1) * LANES)
            move = scale_ref[here, :] * tile_ref[t, here, :]
            out_ref[here, cols] = (amp_ref[here, cols].astype(F32) + move).astype(BF)
        stores.append(pltpu.make_async_copy(out_ref.at[here], out_any.at[here], sem_out.at[j]))
        stores[j].start()
    for cp in stores:
        cp.wait()


def pick(pair_source, interaction, quota):
    blocks, rows_block, width = interaction.shape
    count = quota * LANES
    states = blocks * rows_block
    return call(
        functools.partial(pick_body, quota),
        jax.ShapeDtypeStruct((count + TAGS, width), BF),
        [VM, VM],
        VM,
        [pltpu.VMEM((count, states), BF)],
        name="pick",
    )(pair_source, interaction.reshape(states, width))


def pack(amplitudes, recoupling, orbs, quota):
    rows, width = amplitudes.shape
    tiles = width // LANES
    return call(
        functools.partial(pack_body, orbs, quota),
        pltpu.HBM((rows * tiles, LANES), BF),
        [VM, VM],
        ANY,
        [
            pltpu.VMEM((rows, LANES), F32),
            pltpu.VMEM((tiles, rows, LANES), F32),
            pltpu.VMEM((rows * tiles, LANES), F32),
            pltpu.VMEM((rows * tiles, LANES), BF),
            pltpu.SemaphoreType.DMA((CHUNKS,)),
        ],
        name="pack",
    )(near(amplitudes), recoupling.reshape(rows // LANES, LANES))


def build(here, sizes, own, after, before, far, quota):
    count = quota * LANES
    mixed = pltpu.HBM((count, 4 * count), BF)
    outs = (
        mixed, mixed, mixed,
        pltpu.HBM((4, own.shape[1] // 4, count), BF),
        pltpu.HBM((4, 8, count), F32),
        pltpu.HBM((count, LANES), F32),
        pltpu.HBM((4 * count, LANES), F32),
    )
    return call(
        functools.partial(build_body, quota),
        outs,
        [SM, SM, VM, VM, VM, VM],
        (VM,) * len(outs),
        [pltpu.VMEM((4, TAGS, count), F32)],
        name="build",
    )(here, sizes, own, after, before, far)


def cycle(here, raw, m0, m1, m3, hot, block, owner, limit, quota):
    count = quota * LANES
    return call(
        functools.partial(cycle_body, quota),
        (
            pltpu.VMEM((4 * count, 2 * LANES), BF),
            pltpu.VMEM(raw.shape, F32),
            pltpu.VMEM(hot.shape, BF),
            pltpu.VMEM(block.shape, F32),
            pltpu.VMEM(owner.shape, F32),
        ),
        [SM, VM] + [ANY] * 7,
        (VM,) * 5,
        [
            pltpu.VMEM(raw.shape, F32),
            pltpu.VMEM(limit.shape, F32),
            pltpu.VMEM((3, count, 4 * count), BF),
            pltpu.SemaphoreType.DMA((7,)),
        ],
        name="cycle",
    )(here, near(raw), limit, hot, block, owner, m0, m1, m3)


def close(here, lo, hi, hot, block, owner, rows, flat, quota):
    count = quota * LANES
    out, _ = call(
        functools.partial(close_body, quota),
        (pltpu.VMEM(flat.shape, BF), pltpu.VMEM(flat.shape, F32)),
        [SM] + [VM] * 7,
        (VM, VM),
        [pltpu.VMEM((count, 4 * count), BF)],
        input_output_aliases={7: 1},
        name="close",
    )(here, lo, hi, near(hot), near(block), near(owner), near(rows), near(flat))
    return out


def finish(raw, amplitudes, recoupling, denominators, orbs, quota):
    rows, width = amplitudes.shape
    tiles = width // LANES
    return call(
        functools.partial(finish_body, orbs, quota),
        jax.ShapeDtypeStruct((rows, width), BF),
        [VM, VM, VM, VM],
        ANY,
        [
            pltpu.VMEM((rows, LANES), F32),
            pltpu.VMEM((rows * tiles, LANES), F32),
            pltpu.VMEM((tiles, rows, LANES), F32),
            pltpu.VMEM((rows, width), BF),
            pltpu.SemaphoreType.DMA((CHUNKS,)),
        ],
        name="finish",
    )(
        near(raw), near(amplitudes),
        recoupling.reshape(rows // LANES, LANES), denominators.reshape(rows // LANES, LANES),
    )


def shards(
    amplitudes, recoupling, denominators, interaction, pair_source, return_slot, channel_sizes
):
    chan_count = lax.axis_size("chan")
    orbs = lax.axis_size("orb")
    row_count, _ = amplitudes.shape
    quota = row_count // chan_count
    count = quota * LANES
    half = count // 2
    halves = pair_source.shape[1] // LANES
    peers = chan_count * orbs

    def shift(x, by):
        return lax.ppermute(x, "orb", [(i, (i + by) % orbs) for i in range(orbs)])

    def exchange(x):
        x = x.reshape(peers, quota, halves, LANES)
        x = lax.all_to_all(x, BOTH, split_axis=0, concat_axis=0, tiled=True)
        return x.reshape(peers * quota * halves, LANES)

    own = pick(pair_source, interaction, quota)
    after = shift(own, -1)
    before = shift(own, 1)
    outgoing, _ = lax.optimization_barrier((pack(amplitudes, recoupling, orbs, quota), own))
    raw = exchange(outgoing)
    far = shift(own[count:], 2)
    lo = shift(after[:half], -1)
    hi = shift(before[half:count], 1)
    here = lax.axis_index("orb").astype(jnp.int32).reshape(1)
    m0, m1, m3, hot, block, owner, limit = build(
        here, channel_sizes, own, after, before, far, quota
    )
    rows, flat, hot, block, owner = cycle(
        here, raw, m0, m1, m3, hot, block, owner, limit, quota
    )
    back = close(here, lo, hi, hot, block, owner, rows, flat, quota)
    returned = exchange(back)
    return finish(returned, amplitudes, recoupling, denominators, orbs, quota)


def solution(mesh):
    in_specs = (
        P(("chan", "orb"), None),
        P(("chan", "orb")),
        P(("chan", "orb")),
        P("chan", "orb", None),
        P("chan", "orb"),
        P(("chan", "orb")),
        P("chan"),
    )
    out_specs = P(("chan", "orb"), None)
    return jax.shard_map(
        shards, mesh=mesh, in_specs=in_specs, out_specs=out_specs, check_vma=False
    )
```

```python
import functools

import jax
import jax.numpy as jnp
from jax import lax
from jax.experimental import pallas as pl
from jax.experimental.pallas import tpu as pltpu
from jax.sharding import PartitionSpec as P


BOTH = ("chan", "orb")
LANES = 128
TAGS = 16
BF = jnp.bfloat16
F32 = jnp.float32
VMEM_BYTES = 48 * 1024 * 1024
CHUNKS = 4

VM = pl.BlockSpec(memory_space=pltpu.VMEM)
SM = pl.BlockSpec(memory_space=pltpu.SMEM)
ANY = pl.BlockSpec(memory_space=pl.ANY)


def call(body, out_shape, in_specs, out_specs, scratch=(), **kw):
    return pl.pallas_call(
        body,
        out_shape=out_shape,
        in_specs=in_specs,
        out_specs=out_specs,
        scratch_shapes=list(scratch),
        compiler_params=pltpu.CompilerParams(vmem_limit_bytes=VMEM_BYTES),
        **kw,
    )


def near(x):
    return pltpu.with_memory_space_constraint(x, pltpu.VMEM)


def apart(x):
    return pltpu.with_memory_space_constraint(x, pltpu.HBM)


def one_hot(hit):
    return jnp.where(hit, 1.0, 0.0).astype(BF)


def column(rows):
    r, n = rows.shape
    tall = jnp.concatenate([rows, jnp.zeros((LANES - r, n), F32)], axis=0)
    return jnp.transpose(tall)


def pick_body(quota, src_any, w_any, out_ref, src_ref, w_ref, hit_ref, sem_src, sem_w):
    blocks, rows_block = src_ref.shape
    states, width = w_ref.shape
    count = quota * LANES
    index = pltpu.make_async_copy(src_any, src_ref, sem_src)
    index.start()
    loads = []
    for c in range(blocks):
        at = slice(c * rows_block, (c + 1) * rows_block)
        loads.append(pltpu.make_async_copy(w_any.at[at], w_ref.at[at], sem_w.at[c]))
        loads[c].start()
    index.wait()
    src = jnp.concatenate([src_ref[c : c + 1, :] for c in range(blocks)], axis=1)
    sender = (src * 205) >> 10
    place = jnp.where(src >= 0, (src - sender * quota) * LANES + sender, -1)
    lane = lax.broadcasted_iota(jnp.int32, (TAGS, states), 1)
    which = lax.broadcasted_iota(jnp.int32, (TAGS, states), 0)
    labels = jnp.where(which == 0, lane // rows_block, jnp.where(which == 1, lane % rows_block, 0))
    labels = labels.astype(F32).astype(BF)
    out_ref[count:, count:] = jnp.zeros((TAGS, width - count), BF)
    for q in range(quota):
        at = lax.broadcasted_iota(jnp.int32, (LANES, states), 0) + q * LANES
        hit = one_hot(at == place)
        here = slice(q * LANES, (q + 1) * LANES)
        hit_ref[here, :] = hit
        out_ref[count:, here] = lax.dot_general(
            labels, hit, (((1,), (1,)), ((), ())), preferred_element_type=F32
        ).astype(BF)
    for cp in loads:
        cp.wait()
    out_ref[:count, :] = jnp.dot(
        hit_ref[...], w_ref[...], preferred_element_type=F32
    ).astype(BF)


def spread_rows(value, out_ref):
    tall = column(value)
    for a in range(value.shape[0]):
        out_ref[a * LANES : (a + 1) * LANES, :] = jnp.broadcast_to(
            tall[:, a : a + 1], (LANES, LANES)
        )


def pack_body(
    orbs, quota, amp_ref, rec_ref, out_any, scale_ref, tile_ref, flat_ref, out_ref, sem_out
):
    rows, width = amp_ref.shape
    tiles = width // LANES
    halves = tiles // orbs
    part = rows // CHUNKS
    groups = part // quota
    spread_rows(rec_ref[...], scale_ref)
    stores = []
    for j in range(CHUNKS):
        here = slice(j * part, (j + 1) * part)
        for t in range(tiles):
            tile_ref[t, here, :] = (
                amp_ref[here, t * LANES : (t + 1) * LANES].astype(F32) * scale_ref[here, :]
            )
        for o in range(orbs):
            for q in range(quota):
                for h in range(halves):
                    piece = tile_ref[o * halves + h, pl.ds(j * part + q, groups, stride=quota), :]
                    at = j * part * tiles + (o * quota + q) * halves + h
                    flat_ref[pl.ds(at, groups, stride=orbs * quota * halves), :] = piece
        to = slice(j * part * tiles, (j + 1) * part * tiles)
        out_ref[to, :] = flat_ref[to, :].astype(BF)
        stores.append(pltpu.make_async_copy(out_ref.at[to], out_any.at[to], sem_out.at[j]))
        stores[j].start()
    for cp in stores:
        cp.wait()


def mix(w, hot_ref, block_ref, owner, out_ref):
    orbs, rows_block, count = hot_ref.shape
    for o in range(orbs):
        spread = jnp.dot(
            w[:, o * rows_block : (o + 1) * rows_block], hot_ref[o], preferred_element_type=F32
        )
        out_ref[:, o * count : (o + 1) * count] = jnp.where(
            owner == block_ref[o, 0:1, :], spread, 0.0
        ).astype(BF)


def cycle_body(
    quota, here_ref, size_ref, raw_ref, far_ref, own_any, after_any, before_any,
    rows_ref, flat_ref, hot_ref, block_ref, owner_ref,
    wide_ref, tag_ref, tags_ref, w_ref, mix_ref, sem_tag, sem_w,
):
    orbs, rows_block, count = hot_ref.shape
    halves = rows_block // LANES
    sources = (own_any, after_any, before_any)
    tag_copies = [
        pltpu.make_async_copy(src.at[count:], tag_ref.at[i], sem_tag.at[i])
        for i, src in enumerate(sources)
    ]
    copies = [
        pltpu.make_async_copy(src.at[:count], w_ref.at[i], sem_w.at[i])
        for i, src in enumerate(sources)
    ]
    for cp in tag_copies + copies:
        cp.start()
    here = here_ref[0]
    step = orbs * quota * halves
    lane = lax.broadcasted_iota(jnp.int32, (LANES, LANES), 1).astype(F32)
    slot = lax.broadcasted_iota(jnp.int32, (rows_block, count), 0).astype(F32)
    wide_ref[...] = raw_ref[...].astype(F32)
    for cp in tag_copies:
        cp.wait()
    tags_ref[2] = far_ref[:, :count].astype(F32)
    for i, s in enumerate((0, 1, 3)):
        tags_ref[s] = tag_ref[i, :, :count].astype(F32)
    for o in range(orbs):
        tag = tags_ref[(o + orbs - here) % orbs]
        hot_ref[o] = one_hot(slot == tag[1:2, :])
        block_ref[o] = tag[0:8, :]
        size = jnp.zeros((1, count), F32)
        for c in range(size_ref.shape[0]):
            live = (size_ref[c] // orbs).astype(F32)
            size = size + jnp.where(tag[0:1, :] == float(c), live, 0.0)
        size = column(size)[:, 0:1]
        for q in range(quota):
            row = o * count + q * LANES
            for h in range(halves):
                piece = wide_ref[pl.ds((o * quota + q) * halves + h, LANES, stride=step), :]
                keep = lane + float(h * LANES) < size[q * LANES : (q + 1) * LANES]
                rows_ref[row : row + LANES, h * LANES : (h + 1) * LANES] = jnp.where(
                    keep, piece, 0.0
                ).astype(BF)
    owner_ref[...] = jnp.broadcast_to(column(tags_ref[2])[:, 0:1], (count, LANES))
    for i, s in enumerate((0, 1, 3)):
        copies[i].wait()
        mix(w_ref.at[i], hot_ref, block_ref, column(tags_ref[s])[:, 0:1], mix_ref.at[i])
        scatter(quota, (here + s) % orbs, step, mix_ref[i], rows_ref, flat_ref)


def scatter(quota, to, step, mix, rows_ref, flat_ref):
    halves = rows_ref.shape[1] // LANES
    done = jnp.dot(mix, rows_ref[...], preferred_element_type=F32)
    for q in range(quota):
        for h in range(halves):
            flat_ref[pl.ds((to * quota + q) * halves + h, LANES, stride=step), :] = done[
                q * LANES : (q + 1) * LANES, h * LANES : (h + 1) * LANES
            ]


def close_body(
    quota, here_ref, lo_ref, hi_ref, hot_ref, block_ref, owner_ref, rows_ref, flat_in,
    out_ref, flat_ref, mix_ref,
):
    orbs, rows_block, count = hot_ref.shape
    half = count // 2
    step = orbs * quota * (rows_block // LANES)
    for i, ref in enumerate((lo_ref, hi_ref)):
        at = slice(i * half, (i + 1) * half)
        mix(ref, hot_ref, block_ref, owner_ref[at, 0:1], mix_ref.at[at])
    scatter(quota, (here_ref[0] + 2) % orbs, step, mix_ref[...], rows_ref, flat_ref)
    out_ref[...] = flat_ref[...].astype(BF)


def finish_body(
    orbs, quota, raw_ref, amp_ref, rec_ref, den_ref, out_any,
    scale_ref, flat_ref, tile_ref, out_ref, sem_out,
):
    rows, width = amp_ref.shape
    tiles = width // LANES
    halves = tiles // orbs
    part = rows // CHUNKS
    groups = part // quota
    spread_rows(rec_ref[...] / den_ref[...], scale_ref)
    stores = []
    for j in range(CHUNKS):
        here = slice(j * part, (j + 1) * part)
        to = slice(j * part * tiles, (j + 1) * part * tiles)
        flat_ref[to, :] = raw_ref[to, :].astype(F32)
        for o in range(orbs):
            for q in range(quota):
                for h in range(halves):
                    at = j * part * tiles + (o * quota + q) * halves + h
                    piece = flat_ref[pl.ds(at, groups, stride=orbs * quota * halves), :]
                    tile_ref[o * halves + h, pl.ds(j * part + q, groups, stride=quota), :] = piece
        for t in range(tiles):
            cols = slice(t * LANES, (t + 1) * LANES)
            move = scale_ref[here, :] * tile_ref[t, here, :]
            out_ref[here, cols] = (amp_ref[here, cols].astype(F32) + move).astype(BF)
        stores.append(pltpu.make_async_copy(out_ref.at[here], out_any.at[here], sem_out.at[j]))
        stores[j].start()
    for cp in stores:
        cp.wait()


def pick(pair_source, interaction, quota):
    blocks, rows_block, width = interaction.shape
    count = quota * LANES
    states = blocks * rows_block
    return call(
        functools.partial(pick_body, quota),
        pltpu.VMEM((count + TAGS, width), BF),
        [ANY, ANY],
        VM,
        [
            pltpu.VMEM((blocks, rows_block), jnp.int32),
            pltpu.VMEM((states, width), BF),
            pltpu.VMEM((count, states), BF),
            pltpu.SemaphoreType.DMA,
            pltpu.SemaphoreType.DMA((blocks,)),
        ],
        name="pick",
    )(apart(pair_source), apart(interaction.reshape(states, width)))


def pack(amplitudes, recoupling, orbs, quota):
    rows, width = amplitudes.shape
    tiles = width // LANES
    return call(
        functools.partial(pack_body, orbs, quota),
        pltpu.HBM((rows * tiles, LANES), BF),
        [VM, VM],
        ANY,
        [
            pltpu.VMEM((rows, LANES), F32),
            pltpu.VMEM((tiles, rows, LANES), F32),
            pltpu.VMEM((rows * tiles, LANES), F32),
            pltpu.VMEM((rows * tiles, LANES), BF),
            pltpu.SemaphoreType.DMA((CHUNKS,)),
        ],
        name="pack",
    )(near(amplitudes), recoupling.reshape(rows // LANES, LANES))


def cycle(here, sizes, raw, far, own, after, before, quota):
    count = quota * LANES
    width = own.shape[1]
    return call(
        functools.partial(cycle_body, quota),
        (
            pltpu.VMEM((4 * count, 2 * LANES), BF),
            pltpu.VMEM(raw.shape, F32),
            pltpu.VMEM((4, 2 * LANES, count), BF),
            pltpu.VMEM((4, 8, count), F32),
            pltpu.VMEM((count, LANES), F32),
        ),
        [SM, SM, VM, VM] + [ANY] * 3,
        (VM,) * 5,
        [
            pltpu.VMEM(raw.shape, F32),
            pltpu.VMEM((3, TAGS, width), BF),
            pltpu.VMEM((4, TAGS, count), F32),
            pltpu.VMEM((3, count, width), BF),
            pltpu.VMEM((3, count, 4 * count), BF),
            pltpu.SemaphoreType.DMA((3,)),
            pltpu.SemaphoreType.DMA((3,)),
        ],
        name="cycle",
    )(here, sizes, near(raw), near(far), own, after, before)


def close(here, lo, hi, hot, block, owner, rows, flat, quota):
    count = quota * LANES
    out, _ = call(
        functools.partial(close_body, quota),
        (pltpu.VMEM(flat.shape, BF), pltpu.VMEM(flat.shape, F32)),
        [SM] + [VM] * 7,
        (VM, VM),
        [pltpu.VMEM((count, 4 * count), BF)],
        input_output_aliases={7: 1},
        name="close",
    )(here, apart(lo), apart(hi), near(hot), near(block), near(owner), near(rows), near(flat))
    return out


def finish(raw, amplitudes, recoupling, denominators, orbs, quota):
    rows, width = amplitudes.shape
    tiles = width // LANES
    return call(
        functools.partial(finish_body, orbs, quota),
        jax.ShapeDtypeStruct((rows, width), BF),
        [VM, VM, VM, VM],
        ANY,
        [
            pltpu.VMEM((rows, LANES), F32),
            pltpu.VMEM((rows * tiles, LANES), F32),
            pltpu.VMEM((tiles, rows, LANES), F32),
            pltpu.VMEM((rows, width), BF),
            pltpu.SemaphoreType.DMA((CHUNKS,)),
        ],
        name="finish",
    )(
        near(raw), near(amplitudes),
        recoupling.reshape(rows // LANES, LANES), denominators.reshape(rows // LANES, LANES),
    )


def shards(
    amplitudes, recoupling, denominators, interaction, pair_source, return_slot, channel_sizes
):
    chan_count = lax.axis_size("chan")
    orbs = lax.axis_size("orb")
    row_count, _ = amplitudes.shape
    quota = row_count // chan_count
    count = quota * LANES
    half = count // 2
    halves = pair_source.shape[1] // LANES
    peers = chan_count * orbs

    def shift(x, by):
        return lax.ppermute(x, "orb", [(i, (i + by) % orbs) for i in range(orbs)])

    def exchange(x):
        x = x.reshape(peers, quota, halves, LANES)
        x = lax.all_to_all(x, BOTH, split_axis=0, concat_axis=0, tiled=True)
        return x.reshape(peers * quota * halves, LANES)

    own = pick(pair_source, interaction, quota)
    after = shift(own, -1)
    before = shift(own, 1)
    outgoing, _ = lax.optimization_barrier((pack(amplitudes, recoupling, orbs, quota), own))
    raw = exchange(outgoing)
    far = shift(own[count:], 2)
    lo = shift(after[:half], -1)
    hi = shift(before[half:count], 1)
    here = lax.axis_index("orb").astype(jnp.int32).reshape(1)
    rows, flat, hot, block, owner = cycle(
        here, channel_sizes, raw, far, own, after, before, quota
    )
    back = close(here, lo, hi, hot, block, owner, rows, flat, quota)
    returned = exchange(back)
    return finish(returned, amplitudes, recoupling, denominators, orbs, quota)


def solution(mesh):
    in_specs = (
        P(("chan", "orb"), None),
        P(("chan", "orb")),
        P(("chan", "orb")),
        P("chan", "orb", None),
        P("chan", "orb"),
        P(("chan", "orb")),
        P("chan"),
    )
    out_specs = P(("chan", "orb"), None)
    return jax.shard_map(
        shards, mesh=mesh, in_specs=in_specs, out_specs=out_specs, check_vma=False
    )
```

```python
import functools

import jax
import jax.numpy as jnp
from jax import lax
from jax.experimental import pallas as pl
from jax.experimental.pallas import tpu as pltpu
from jax.sharding import PartitionSpec as P


BOTH = ("chan", "orb")
LANES = 128
TAGS = 16
BF = jnp.bfloat16
F32 = jnp.float32
VMEM_BYTES = 48 * 1024 * 1024
CHUNKS = 4

VM = pl.BlockSpec(memory_space=pltpu.VMEM)
SM = pl.BlockSpec(memory_space=pltpu.SMEM)
ANY = pl.BlockSpec(memory_space=pl.ANY)


def call(body, out_shape, in_specs, out_specs, scratch=(), **kw):
    return pl.pallas_call(
        body,
        out_shape=out_shape,
        in_specs=in_specs,
        out_specs=out_specs,
        scratch_shapes=list(scratch),
        compiler_params=pltpu.CompilerParams(vmem_limit_bytes=VMEM_BYTES),
        **kw,
    )


def near(x):
    return pltpu.with_memory_space_constraint(x, pltpu.VMEM)


def apart(x):
    return pltpu.with_memory_space_constraint(x, pltpu.HBM)


def one_hot(hit):
    return jnp.where(hit, 1.0, 0.0).astype(BF)


def column(rows):
    r, n = rows.shape
    tall = jnp.concatenate([rows, jnp.zeros((LANES - r, n), F32)], axis=0)
    return jnp.transpose(tall)


def pick_body(quota, src_any, w_any, out_ref, src_ref, w_ref, hit_ref, sem_src, sem_w):
    blocks, rows_block = src_ref.shape
    states, width = w_ref.shape
    count = quota * LANES
    index = pltpu.make_async_copy(src_any, src_ref, sem_src)
    index.start()
    loads = []
    for c in range(blocks):
        at = slice(c * rows_block, (c + 1) * rows_block)
        loads.append(pltpu.make_async_copy(w_any.at[at], w_ref.at[at], sem_w.at[c]))
        loads[c].start()
    index.wait()
    src = jnp.concatenate([src_ref[c : c + 1, :] for c in range(blocks)], axis=1)
    sender = (src * 205) >> 10
    place = jnp.where(src >= 0, (src - sender * quota) * LANES + sender, -1)
    state = lax.broadcasted_iota(jnp.int32, (states, LANES), 0)
    which = lax.broadcasted_iota(jnp.int32, (states, LANES), 1)
    labels = jnp.where(
        which == 0, state // rows_block, jnp.where(which == 1, state % rows_block, 0)
    )
    labels = labels.astype(F32).astype(BF)
    for q in range(quota):
        at = lax.broadcasted_iota(jnp.int32, (LANES, states), 0) + q * LANES
        hit_ref[q * LANES : (q + 1) * LANES, :] = one_hot(at == place)
    tags = jnp.transpose(jnp.dot(hit_ref[...], labels, preferred_element_type=F32))
    out_ref[count:, count:] = jnp.zeros((TAGS, width - count), BF)
    out_ref[count:, :count] = tags[:TAGS].astype(BF)
    for cp in loads:
        cp.wait()
    out_ref[:count, :] = jnp.dot(
        hit_ref[...], w_ref[...], preferred_element_type=F32
    ).astype(BF)


def spread_rows(value, out_ref):
    tall = column(value)
    for a in range(value.shape[0]):
        out_ref[a * LANES : (a + 1) * LANES, :] = jnp.broadcast_to(
            tall[:, a : a + 1], (LANES, LANES)
        )


def pack_body(
    orbs, quota, amp_ref, rec_ref, out_any, scale_ref, tile_ref, flat_ref, out_ref, sem_out
):
    rows, width = amp_ref.shape
    tiles = width // LANES
    halves = tiles // orbs
    part = rows // CHUNKS
    groups = part // quota
    spread_rows(rec_ref[...], scale_ref)
    stores = []
    for j in range(CHUNKS):
        here = slice(j * part, (j + 1) * part)
        for t in range(tiles):
            tile_ref[t, here, :] = (
                amp_ref[here, t * LANES : (t + 1) * LANES].astype(F32) * scale_ref[here, :]
            )
        for o in range(orbs):
            for q in range(quota):
                for h in range(halves):
                    piece = tile_ref[o * halves + h, pl.ds(j * part + q, groups, stride=quota), :]
                    at = j * part * tiles + (o * quota + q) * halves + h
                    flat_ref[pl.ds(at, groups, stride=orbs * quota * halves), :] = piece
        to = slice(j * part * tiles, (j + 1) * part * tiles)
        out_ref[to, :] = flat_ref[to, :].astype(BF)
        stores.append(pltpu.make_async_copy(out_ref.at[to], out_any.at[to], sem_out.at[j]))
        stores[j].start()
    for cp in stores:
        cp.wait()


def mix(w, hot_ref, block_ref, owner, out_ref):
    orbs, rows_block, count = hot_ref.shape
    for o in range(orbs):
        spread = jnp.dot(
            w[:, o * rows_block : (o + 1) * rows_block], hot_ref[o], preferred_element_type=F32
        )
        out_ref[:, o * count : (o + 1) * count] = jnp.where(
            owner == block_ref[o, 0:1, :], spread.astype(BF), jnp.zeros((), BF)
        )


def cycle_body(
    quota, here_ref, size_ref, raw_any, far_ref, own_any, after_any, before_any,
    rows_ref, flat_ref, hot_ref, block_ref, owner_ref,
    raw_ref, wide_ref, tag_ref, tags_ref, w_ref, mix_ref, sem_tag, sem_w,
):
    orbs, rows_block, count = hot_ref.shape
    halves = rows_block // LANES
    sources = (own_any, after_any, before_any)
    tag_copies = [
        pltpu.make_async_copy(src.at[count:], tag_ref.at[i], sem_tag.at[i])
        for i, src in enumerate(sources)
    ]
    copies = [
        pltpu.make_async_copy(src.at[:count], w_ref.at[i], sem_w.at[i])
        for i, src in enumerate(sources)
    ]
    raw_copy = pltpu.make_async_copy(raw_any, raw_ref, sem_w.at[3])
    for cp in (*tag_copies, raw_copy, *copies):
        cp.start()
    here = here_ref[0]
    step = orbs * quota * halves
    lane = lax.broadcasted_iota(jnp.int32, (LANES, LANES), 1).astype(F32)
    slot = lax.broadcasted_iota(jnp.int32, (rows_block, count), 0).astype(F32).astype(BF)
    for cp in tag_copies:
        cp.wait()
    tags_ref[2] = far_ref[:, :count]
    for i, s in enumerate((0, 1, 3)):
        tags_ref[s] = tag_ref[i, :, :count]
    sizes = []
    for o in range(orbs):
        tag = tags_ref[(o + orbs - here) % orbs]
        hot_ref[o] = jnp.where(slot == tag[1:2, :], jnp.ones((), BF), jnp.zeros((), BF))
        block_ref[o] = tag
        blocks = tag[0:1, :].astype(F32)
        size = jnp.zeros((1, count), F32)
        for c in range(size_ref.shape[0]):
            live = (size_ref[c] // orbs).astype(F32)
            size = size + jnp.where(blocks == float(c), live, 0.0)
        sizes.append(size)
    sizes = column(jnp.concatenate(sizes, axis=0))
    owners = column(jnp.concatenate([tags_ref[s, 0:1, :].astype(F32) for s in range(orbs)], axis=0))
    owner_ref[...] = jnp.broadcast_to(owners[:, 2:3], (count, LANES)).astype(BF)
    raw_copy.wait()
    wide_ref[...] = raw_ref[...].astype(F32)
    for o in range(orbs):
        for q in range(quota):
            row = o * count + q * LANES
            size = sizes[q * LANES : (q + 1) * LANES, o : o + 1]
            for h in range(halves):
                piece = wide_ref[pl.ds((o * quota + q) * halves + h, LANES, stride=step), :]
                rows_ref[row : row + LANES, h * LANES : (h + 1) * LANES] = jnp.where(
                    lane + float(h * LANES) < size, piece, 0.0
                ).astype(BF)
    for i, s in enumerate((0, 1, 3)):
        copies[i].wait()
        owner = jnp.broadcast_to(owners[:, s : s + 1], (count, LANES)).astype(BF)
        mix(w_ref.at[i], hot_ref, block_ref, owner[:, 0:1], mix_ref.at[i])
        scatter(quota, (here + s) % orbs, step, mix_ref[i], rows_ref, flat_ref)


def scatter(quota, to, step, mix, rows_ref, flat_ref):
    halves = rows_ref.shape[1] // LANES
    done = jnp.dot(mix, rows_ref[...], preferred_element_type=F32)
    for q in range(quota):
        for h in range(halves):
            flat_ref[pl.ds((to * quota + q) * halves + h, LANES, stride=step), :] = done[
                q * LANES : (q + 1) * LANES, h * LANES : (h + 1) * LANES
            ]


def close_body(
    quota, here_ref, lo_any, hi_ref, hot_ref, block_ref, owner_ref, rows_ref, flat_in,
    out_ref, flat_ref, lo_ref, mix_ref, sem,
):
    orbs, rows_block, count = hot_ref.shape
    half = count // 2
    step = orbs * quota * (rows_block // LANES)
    load = pltpu.make_async_copy(lo_any, lo_ref, sem)
    load.start()
    mix(hi_ref, hot_ref, block_ref, owner_ref[half:, 0:1], mix_ref.at[half:])
    load.wait()
    mix(lo_ref, hot_ref, block_ref, owner_ref[:half, 0:1], mix_ref.at[:half])
    scatter(quota, (here_ref[0] + 2) % orbs, step, mix_ref[...], rows_ref, flat_ref)
    out_ref[...] = flat_ref[...].astype(BF)


def finish_body(
    orbs, quota, raw_ref, amp_ref, rec_ref, den_ref, out_any,
    scale_ref, flat_ref, tile_ref, out_ref, sem_out,
):
    rows, width = amp_ref.shape
    tiles = width // LANES
    halves = tiles // orbs
    part = rows // CHUNKS
    groups = part // quota
    spread_rows(rec_ref[...] / den_ref[...], scale_ref)
    stores = []
    for j in range(CHUNKS):
        here = slice(j * part, (j + 1) * part)
        to = slice(j * part * tiles, (j + 1) * part * tiles)
        flat_ref[to, :] = raw_ref[to, :].astype(F32)
        for o in range(orbs):
            for q in range(quota):
                for h in range(halves):
                    at = j * part * tiles + (o * quota + q) * halves + h
                    piece = flat_ref[pl.ds(at, groups, stride=orbs * quota * halves), :]
                    tile_ref[o * halves + h, pl.ds(j * part + q, groups, stride=quota), :] = piece
        for t in range(tiles):
            cols = slice(t * LANES, (t + 1) * LANES)
            move = scale_ref[here, :] * tile_ref[t, here, :]
            out_ref[here, cols] = (amp_ref[here, cols].astype(F32) + move).astype(BF)
        stores.append(pltpu.make_async_copy(out_ref.at[here], out_any.at[here], sem_out.at[j]))
        stores[j].start()
    for cp in stores:
        cp.wait()


def pick(pair_source, interaction, quota):
    blocks, rows_block, width = interaction.shape
    count = quota * LANES
    states = blocks * rows_block
    return call(
        functools.partial(pick_body, quota),
        pltpu.VMEM((count + TAGS, width), BF),
        [ANY, ANY],
        VM,
        [
            pltpu.VMEM((blocks, rows_block), jnp.int32),
            pltpu.VMEM((states, width), BF),
            pltpu.VMEM((count, states), BF),
            pltpu.SemaphoreType.DMA,
            pltpu.SemaphoreType.DMA((blocks,)),
        ],
        name="pick",
    )(apart(pair_source), apart(interaction.reshape(states, width)))


def pack(amplitudes, recoupling, orbs, quota):
    rows, width = amplitudes.shape
    tiles = width // LANES
    return call(
        functools.partial(pack_body, orbs, quota),
        pltpu.HBM((rows * tiles, LANES), BF),
        [VM, VM],
        ANY,
        [
            pltpu.VMEM((rows, LANES), F32),
            pltpu.VMEM((tiles, rows, LANES), F32),
            pltpu.VMEM((rows * tiles, LANES), F32),
            pltpu.VMEM((rows * tiles, LANES), BF),
            pltpu.SemaphoreType.DMA((CHUNKS,)),
        ],
        name="pack",
    )(near(amplitudes), recoupling.reshape(rows // LANES, LANES))


def cycle(here, sizes, raw, far, own, after, before, quota):
    count = quota * LANES
    width = own.shape[1]
    return call(
        functools.partial(cycle_body, quota),
        (
            pltpu.VMEM((4 * count, 2 * LANES), BF),
            pltpu.VMEM(raw.shape, F32),
            pltpu.VMEM((4, 2 * LANES, count), BF),
            pltpu.VMEM((4, TAGS, count), BF),
            pltpu.VMEM((count, LANES), BF),
        ),
        [SM, SM, ANY, VM] + [ANY] * 3,
        (VM,) * 5,
        [
            pltpu.VMEM(raw.shape, BF),
            pltpu.VMEM(raw.shape, F32),
            pltpu.VMEM((3, TAGS, width), BF),
            pltpu.VMEM((4, TAGS, count), BF),
            pltpu.VMEM((3, count, width), BF),
            pltpu.VMEM((3, count, 4 * count), BF),
            pltpu.SemaphoreType.DMA((3,)),
            pltpu.SemaphoreType.DMA((4,)),
        ],
        name="cycle",
    )(here, sizes, raw, far, own, after, before)


def close(here, lo, hi, hot, block, owner, rows, flat, quota):
    count = quota * LANES
    out, _ = call(
        functools.partial(close_body, quota),
        (pltpu.VMEM(flat.shape, BF), pltpu.VMEM(flat.shape, F32)),
        [SM, ANY] + [VM] * 6,
        (VM, VM),
        [
            pltpu.VMEM(lo.shape, BF),
            pltpu.VMEM((count, 4 * count), BF),
            pltpu.SemaphoreType.DMA,
        ],
        input_output_aliases={7: 1},
        name="close",
    )(here, apart(lo), near(hi), near(hot), near(block), near(owner), near(rows), near(flat))
    return out


def finish(raw, amplitudes, recoupling, denominators, orbs, quota):
    rows, width = amplitudes.shape
    tiles = width // LANES
    return call(
        functools.partial(finish_body, orbs, quota),
        jax.ShapeDtypeStruct((rows, width), BF),
        [VM, VM, VM, VM],
        ANY,
        [
            pltpu.VMEM((rows, LANES), F32),
            pltpu.VMEM((rows * tiles, LANES), F32),
            pltpu.VMEM((tiles, rows, LANES), F32),
            pltpu.VMEM((rows, width), BF),
            pltpu.SemaphoreType.DMA((CHUNKS,)),
        ],
        name="finish",
    )(
        near(raw), near(amplitudes),
        recoupling.reshape(rows // LANES, LANES), denominators.reshape(rows // LANES, LANES),
    )


def shards(
    amplitudes, recoupling, denominators, interaction, pair_source, return_slot, channel_sizes
):
    chan_count = lax.axis_size("chan")
    orbs = lax.axis_size("orb")
    row_count, _ = amplitudes.shape
    quota = row_count // chan_count
    count = quota * LANES
    half = count // 2
    halves = pair_source.shape[1] // LANES
    peers = chan_count * orbs

    def shift(x, by):
        return lax.ppermute(x, "orb", [(i, (i + by) % orbs) for i in range(orbs)])

    def exchange(x):
        x = x.reshape(peers, quota, halves, LANES)
        x = lax.all_to_all(x, BOTH, split_axis=0, concat_axis=0, tiled=True)
        return x.reshape(peers * quota * halves, LANES)

    own = pick(pair_source, interaction, quota)
    after = shift(own, -1)
    before = shift(own, 1)
    outgoing, _ = lax.optimization_barrier((pack(amplitudes, recoupling, orbs, quota), own))
    raw = exchange(outgoing)
    far = shift(own[count:], 2)
    lo = shift(after[:half], -1)
    hi = shift(before[half:count], 1)
    here = lax.axis_index("orb").astype(jnp.int32).reshape(1)
    rows, flat, hot, block, owner = cycle(
        here, channel_sizes, raw, far, own, after, before, quota
    )
    back = close(here, lo, hi, hot, block, owner, rows, flat, quota)
    returned = exchange(back)
    return finish(returned, amplitudes, recoupling, denominators, orbs, quota)


def solution(mesh):
    in_specs = (
        P(("chan", "orb"), None),
        P(("chan", "orb")),
        P(("chan", "orb")),
        P("chan", "orb", None),
        P("chan", "orb"),
        P(("chan", "orb")),
        P("chan"),
    )
    out_specs = P(("chan", "orb"), None)
    return jax.shard_map(
        shards, mesh=mesh, in_specs=in_specs, out_specs=out_specs, check_vma=False
    )
```

```python
import functools

import jax
import jax.numpy as jnp
from jax import lax
from jax.experimental import pallas as pl
from jax.experimental.pallas import tpu as pltpu
from jax.sharding import PartitionSpec as P


BOTH = ("chan", "orb")
LANES = 128
TAGS = 16
BF = jnp.bfloat16
F32 = jnp.float32
VMEM_BYTES = 48 * 1024 * 1024
CHUNKS = 4

VM = pl.BlockSpec(memory_space=pltpu.VMEM)
SM = pl.BlockSpec(memory_space=pltpu.SMEM)
ANY = pl.BlockSpec(memory_space=pl.ANY)


def call(body, out_shape, in_specs, out_specs, scratch=(), **kw):
    return pl.pallas_call(
        body,
        out_shape=out_shape,
        in_specs=in_specs,
        out_specs=out_specs,
        scratch_shapes=list(scratch),
        compiler_params=pltpu.CompilerParams(vmem_limit_bytes=VMEM_BYTES),
        **kw,
    )


def near(x):
    return pltpu.with_memory_space_constraint(x, pltpu.VMEM)


def apart(x):
    return pltpu.with_memory_space_constraint(x, pltpu.HBM)


def one_hot(hit):
    return jnp.where(hit, 1.0, 0.0).astype(BF)


def column(rows):
    r, n = rows.shape
    tall = jnp.concatenate([rows, jnp.zeros((LANES - r, n), F32)], axis=0)
    return jnp.transpose(tall)


def pick_body(quota, src_any, w_any, out_ref, src_ref, w_ref, hit_ref, sem_src, sem_w):
    blocks, rows_block = src_ref.shape
    states, width = w_ref.shape
    count = quota * LANES
    index = pltpu.make_async_copy(src_any, src_ref, sem_src)
    index.start()
    loads = []
    for c in range(blocks):
        at = slice(c * rows_block, (c + 1) * rows_block)
        loads.append(pltpu.make_async_copy(w_any.at[at], w_ref.at[at], sem_w.at[c]))
        loads[c].start()
    index.wait()
    src = jnp.concatenate([src_ref[c : c + 1, :] for c in range(blocks)], axis=1)
    sender = (src * 205) >> 10
    place = jnp.where(src >= 0, (src - sender * quota) * LANES + sender, -1)
    state = lax.broadcasted_iota(jnp.int32, (states, LANES), 0)
    which = lax.broadcasted_iota(jnp.int32, (states, LANES), 1)
    labels = jnp.where(
        which == 0, state // rows_block, jnp.where(which == 1, state % rows_block, 0)
    )
    labels = labels.astype(F32).astype(BF)
    for q in range(quota):
        at = lax.broadcasted_iota(jnp.int32, (LANES, states), 0) + q * LANES
        hit_ref[q * LANES : (q + 1) * LANES, :] = one_hot(at == place)
    tags = jnp.transpose(jnp.dot(hit_ref[...], labels, preferred_element_type=F32))
    out_ref[count:, count:] = jnp.zeros((TAGS, width - count), BF)
    out_ref[count:, :count] = tags[:TAGS].astype(BF)
    for cp in loads:
        cp.wait()
    out_ref[:count, :] = jnp.dot(
        hit_ref[...], w_ref[...], preferred_element_type=F32
    ).astype(BF)


def spread_rows(value, out_ref):
    tall = column(value)
    for a in range(value.shape[0]):
        out_ref[a * LANES : (a + 1) * LANES, :] = jnp.broadcast_to(
            tall[:, a : a + 1], (LANES, LANES)
        )


def pack_body(
    orbs, quota, amp_ref, rec_ref, out_any, scale_ref, tile_ref, flat_ref, out_ref, sem_out
):
    rows, width = amp_ref.shape
    tiles = width // LANES
    halves = tiles // orbs
    part = rows // CHUNKS
    groups = part // quota
    spread_rows(rec_ref[...], scale_ref)
    stores = []
    for j in range(CHUNKS):
        here = slice(j * part, (j + 1) * part)
        for t in range(tiles):
            tile_ref[t, here, :] = (
                amp_ref[here, t * LANES : (t + 1) * LANES].astype(F32) * scale_ref[here, :]
            )
        for o in range(orbs):
            for q in range(quota):
                for h in range(halves):
                    piece = tile_ref[o * halves + h, pl.ds(j * part + q, groups, stride=quota), :]
                    at = j * part * tiles + (o * quota + q) * halves + h
                    flat_ref[pl.ds(at, groups, stride=orbs * quota * halves), :] = piece
        to = slice(j * part * tiles, (j + 1) * part * tiles)
        out_ref[to, :] = flat_ref[to, :].astype(BF)
        stores.append(pltpu.make_async_copy(out_ref.at[to], out_any.at[to], sem_out.at[j]))
        stores[j].start()
    for cp in stores:
        cp.wait()


def mix(w, hot_ref, block_ref, owner, out_ref):
    orbs, rows_block, count = hot_ref.shape
    for o in range(orbs):
        spread = jnp.dot(
            w[:, o * rows_block : (o + 1) * rows_block], hot_ref[o], preferred_element_type=F32
        )
        out_ref[:, o * count : (o + 1) * count] = jnp.where(
            owner == block_ref[o, 0:1, :], spread.astype(BF), jnp.zeros((), BF)
        )


def cycle_body(
    quota, here_ref, size_ref, raw_any, far_ref, own_any, after_any, before_any,
    rows_ref, flat_ref, hot_ref, block_ref, owner_ref,
    raw_ref, wide_ref, tag_ref, tags_ref, w_ref, mix_ref, sem_tag, sem_w,
):
    orbs, rows_block, count = hot_ref.shape
    halves = rows_block // LANES
    sources = (own_any, after_any, before_any)
    tag_copies = [
        pltpu.make_async_copy(src.at[count:], tag_ref.at[i], sem_tag.at[i])
        for i, src in enumerate(sources)
    ]
    copies = [
        pltpu.make_async_copy(src.at[:count], w_ref.at[i], sem_w.at[i])
        for i, src in enumerate(sources)
    ]
    raw_copy = pltpu.make_async_copy(raw_any, raw_ref, sem_w.at[3])
    for cp in (*tag_copies, raw_copy, *copies):
        cp.start()
    here = here_ref[0]
    step = orbs * quota * halves
    lane = lax.broadcasted_iota(jnp.int32, (LANES, LANES), 1).astype(F32)
    slot = lax.broadcasted_iota(jnp.int32, (rows_block, count), 0).astype(F32).astype(BF)
    for cp in tag_copies:
        cp.wait()
    tags_ref[2] = far_ref[:, :count]
    for i, s in enumerate((0, 1, 3)):
        tags_ref[s] = tag_ref[i, :, :count]
    sizes = []
    for o in range(orbs):
        tag = tags_ref[(o + orbs - here) % orbs]
        hot_ref[o] = jnp.where(slot == tag[1:2, :], jnp.ones((), BF), jnp.zeros((), BF))
        block_ref[o] = tag
        blocks = tag[0:1, :].astype(F32)
        size = jnp.zeros((1, count), F32)
        for c in range(size_ref.shape[0]):
            live = (size_ref[c] // orbs).astype(F32)
            size = size + jnp.where(blocks == float(c), live, 0.0)
        sizes.append(size)
    sizes = column(jnp.concatenate(sizes, axis=0))
    owners = column(jnp.concatenate([tags_ref[s, 0:1, :].astype(F32) for s in range(orbs)], axis=0))
    owner_ref[...] = jnp.broadcast_to(owners[:, 2:3], (count, LANES)).astype(BF)
    raw_copy.wait()
    wide_ref[...] = raw_ref[...].astype(F32)
    for o in range(orbs):
        for q in range(quota):
            row = o * count + q * LANES
            size = sizes[q * LANES : (q + 1) * LANES, o : o + 1]
            for h in range(halves):
                piece = wide_ref[pl.ds((o * quota + q) * halves + h, LANES, stride=step), :]
                rows_ref[row : row + LANES, h * LANES : (h + 1) * LANES] = jnp.where(
                    lane + float(h * LANES) < size, piece, 0.0
                ).astype(BF)
    for i, s in enumerate((0, 1, 3)):
        copies[i].wait()
        owner = jnp.broadcast_to(owners[:, s : s + 1], (count, LANES)).astype(BF)
        mix(w_ref.at[i], hot_ref, block_ref, owner[:, 0:1], mix_ref.at[i])
        scatter(quota, (here + s) % orbs, step, mix_ref[i], rows_ref, flat_ref)


def scatter(quota, to, step, mix, rows_ref, flat_ref):
    halves = rows_ref.shape[1] // LANES
    done = jnp.dot(mix, rows_ref[...], preferred_element_type=F32)
    for q in range(quota):
        for h in range(halves):
            flat_ref[pl.ds((to * quota + q) * halves + h, LANES, stride=step), :] = done[
                q * LANES : (q + 1) * LANES, h * LANES : (h + 1) * LANES
            ]


def close_body(
    quota, here_ref, lo_any, hi_ref, hot_ref, block_ref, owner_ref, rows_ref, flat_in,
    out_ref, flat_ref, lo_ref, mix_ref, sem,
):
    orbs, rows_block, _ = hot_ref.shape
    half = lo_ref.shape[0]
    step = orbs * quota * (rows_block // LANES)
    load = pltpu.make_async_copy(lo_any, lo_ref, sem)
    load.start()
    mix(hi_ref, hot_ref, block_ref, owner_ref[half:, 0:1], mix_ref.at[half:])
    load.wait()
    mix(lo_ref, hot_ref, block_ref, owner_ref[:half, 0:1], mix_ref.at[:half])
    scatter(quota, (here_ref[0] + 2) % orbs, step, mix_ref[...], rows_ref, flat_ref)
    out_ref[...] = flat_ref[...].astype(BF)


def finish_body(
    orbs, quota, raw_ref, amp_ref, rec_ref, den_ref, out_any,
    scale_ref, flat_ref, tile_ref, out_ref, sem_out,
):
    rows, width = amp_ref.shape
    tiles = width // LANES
    halves = tiles // orbs
    part = rows // CHUNKS
    groups = part // quota
    spread_rows(rec_ref[...] / den_ref[...], scale_ref)
    stores = []
    for j in range(CHUNKS):
        here = slice(j * part, (j + 1) * part)
        to = slice(j * part * tiles, (j + 1) * part * tiles)
        flat_ref[to, :] = raw_ref[to, :].astype(F32)
        for o in range(orbs):
            for q in range(quota):
                for h in range(halves):
                    at = j * part * tiles + (o * quota + q) * halves + h
                    piece = flat_ref[pl.ds(at, groups, stride=orbs * quota * halves), :]
                    tile_ref[o * halves + h, pl.ds(j * part + q, groups, stride=quota), :] = piece
        for t in range(tiles):
            cols = slice(t * LANES, (t + 1) * LANES)
            move = scale_ref[here, :] * tile_ref[t, here, :]
            out_ref[here, cols] = (amp_ref[here, cols].astype(F32) + move).astype(BF)
        stores.append(pltpu.make_async_copy(out_ref.at[here], out_any.at[here], sem_out.at[j]))
        stores[j].start()
    for cp in stores:
        cp.wait()


def pick(pair_source, interaction, quota):
    blocks, rows_block, width = interaction.shape
    count = quota * LANES
    states = blocks * rows_block
    return call(
        functools.partial(pick_body, quota),
        pltpu.VMEM((count + TAGS, width), BF),
        [ANY, ANY],
        VM,
        [
            pltpu.VMEM((blocks, rows_block), jnp.int32),
            pltpu.VMEM((states, width), BF),
            pltpu.VMEM((count, states), BF),
            pltpu.SemaphoreType.DMA,
            pltpu.SemaphoreType.DMA((blocks,)),
        ],
        name="pick",
    )(apart(pair_source), apart(interaction.reshape(states, width)))


def pack(amplitudes, recoupling, orbs, quota):
    rows, width = amplitudes.shape
    tiles = width // LANES
    return call(
        functools.partial(pack_body, orbs, quota),
        pltpu.HBM((rows * tiles, LANES), BF),
        [VM, VM],
        ANY,
        [
            pltpu.VMEM((rows, LANES), F32),
            pltpu.VMEM((tiles, rows, LANES), F32),
            pltpu.VMEM((rows * tiles, LANES), F32),
            pltpu.VMEM((rows * tiles, LANES), BF),
            pltpu.SemaphoreType.DMA((CHUNKS,)),
        ],
        name="pack",
    )(near(amplitudes), recoupling.reshape(rows // LANES, LANES))


def cycle(here, sizes, raw, far, own, after, before, quota):
    count = quota * LANES
    width = own.shape[1]
    return call(
        functools.partial(cycle_body, quota),
        (
            pltpu.VMEM((4 * count, 2 * LANES), BF),
            pltpu.VMEM(raw.shape, F32),
            pltpu.VMEM((4, 2 * LANES, count), BF),
            pltpu.VMEM((4, TAGS, count), BF),
            pltpu.VMEM((count, LANES), BF),
        ),
        [SM, SM, ANY, VM] + [ANY] * 3,
        (VM,) * 5,
        [
            pltpu.VMEM(raw.shape, BF),
            pltpu.VMEM(raw.shape, F32),
            pltpu.VMEM((3, TAGS, width), BF),
            pltpu.VMEM((4, TAGS, count), BF),
            pltpu.VMEM((3, count, width), BF),
            pltpu.VMEM((3, count, 4 * count), BF),
            pltpu.SemaphoreType.DMA((3,)),
            pltpu.SemaphoreType.DMA((4,)),
        ],
        name="cycle",
    )(here, sizes, raw, far, own, after, before)


def close(here, lo, hi, hot, block, owner, rows, flat, quota):
    count = quota * LANES
    out, _ = call(
        functools.partial(close_body, quota),
        (pltpu.VMEM(flat.shape, BF), pltpu.VMEM(flat.shape, F32)),
        [SM, ANY] + [VM] * 6,
        (VM, VM),
        [
            pltpu.VMEM(lo.shape, BF),
            pltpu.VMEM((count, 4 * count), BF),
            pltpu.SemaphoreType.DMA,
        ],
        input_output_aliases={7: 1},
        name="close",
    )(here, apart(lo), near(hi), near(hot), near(block), near(owner), near(rows), near(flat))
    return out


def finish(raw, amplitudes, recoupling, denominators, orbs, quota):
    rows, width = amplitudes.shape
    tiles = width // LANES
    return call(
        functools.partial(finish_body, orbs, quota),
        jax.ShapeDtypeStruct((rows, width), BF),
        [VM, VM, VM, VM],
        ANY,
        [
            pltpu.VMEM((rows, LANES), F32),
            pltpu.VMEM((rows * tiles, LANES), F32),
            pltpu.VMEM((tiles, rows, LANES), F32),
            pltpu.VMEM((rows, width), BF),
            pltpu.SemaphoreType.DMA((CHUNKS,)),
        ],
        name="finish",
    )(
        near(raw), near(amplitudes),
        recoupling.reshape(rows // LANES, LANES), denominators.reshape(rows // LANES, LANES),
    )


def shards(
    amplitudes, recoupling, denominators, interaction, pair_source, return_slot, channel_sizes
):
    chan_count = lax.axis_size("chan")
    orbs = lax.axis_size("orb")
    row_count, _ = amplitudes.shape
    quota = row_count // chan_count
    count = quota * LANES
    early = count * 23 // 40
    halves = pair_source.shape[1] // LANES
    peers = chan_count * orbs

    def shift(x, by):
        return lax.ppermute(x, "orb", [(i, (i + by) % orbs) for i in range(orbs)])

    def exchange(x):
        x = x.reshape(peers, quota, halves, LANES)
        x = lax.all_to_all(x, BOTH, split_axis=0, concat_axis=0, tiled=True)
        return x.reshape(peers * quota * halves, LANES)

    own = pick(pair_source, interaction, quota)
    after = shift(own, -1)
    before = shift(own, 1)
    outgoing, _ = lax.optimization_barrier((pack(amplitudes, recoupling, orbs, quota), own))
    raw = exchange(outgoing)
    far = shift(own[count:], 2)
    lo = shift(after[:early], -1)
    hi = shift(before[early:count], 1)
    here = lax.axis_index("orb").astype(jnp.int32).reshape(1)
    rows, flat, hot, block, owner = cycle(
        here, channel_sizes, raw, far, own, after, before, quota
    )
    back = close(here, lo, hi, hot, block, owner, rows, flat, quota)
    returned = exchange(back)
    return finish(returned, amplitudes, recoupling, denominators, orbs, quota)


def solution(mesh):
    in_specs = (
        P(("chan", "orb"), None),
        P(("chan", "orb")),
        P(("chan", "orb")),
        P("chan", "orb", None),
        P("chan", "orb"),
        P(("chan", "orb")),
        P("chan"),
    )
    out_specs = P(("chan", "orb"), None)
    return jax.shard_map(
        shards, mesh=mesh, in_specs=in_specs, out_specs=out_specs, check_vma=False
    )
```

```python
import functools

import jax
import jax.numpy as jnp
from jax import lax
from jax.experimental import pallas as pl
from jax.experimental.pallas import tpu as pltpu
from jax.sharding import PartitionSpec as P


BOTH = ("chan", "orb")
LANES = 128
TAGS = 16
BF = jnp.bfloat16
F32 = jnp.float32
VMEM_BYTES = 48 * 1024 * 1024
CHUNKS = 4

VM = pl.BlockSpec(memory_space=pltpu.VMEM)
SM = pl.BlockSpec(memory_space=pltpu.SMEM)
ANY = pl.BlockSpec(memory_space=pl.ANY)


def call(body, out_shape, in_specs, out_specs, scratch=(), **kw):
    return pl.pallas_call(
        body,
        out_shape=out_shape,
        in_specs=in_specs,
        out_specs=out_specs,
        scratch_shapes=list(scratch),
        compiler_params=pltpu.CompilerParams(vmem_limit_bytes=VMEM_BYTES),
        **kw,
    )


def near(x):
    return pltpu.with_memory_space_constraint(x, pltpu.VMEM)


def apart(x):
    return pltpu.with_memory_space_constraint(x, pltpu.HBM)


def one_hot(hit):
    return jnp.where(hit, 1.0, 0.0).astype(BF)


def column(rows):
    r, n = rows.shape
    tall = jnp.concatenate([rows, jnp.zeros((LANES - r, n), F32)], axis=0)
    return jnp.transpose(tall)


def pick_body(quota, src_any, w_any, out_ref, src_ref, w_ref, hit_ref, sem_src, sem_w):
    blocks, rows_block = src_ref.shape
    states, width = w_ref.shape
    count = quota * LANES
    index = pltpu.make_async_copy(src_any, src_ref, sem_src)
    index.start()
    loads = []
    for c in range(blocks):
        at = slice(c * rows_block, (c + 1) * rows_block)
        loads.append(pltpu.make_async_copy(w_any.at[at], w_ref.at[at], sem_w.at[c]))
        loads[c].start()
    index.wait()
    src = jnp.concatenate([src_ref[c : c + 1, :] for c in range(blocks)], axis=1)
    sender = (src * 205) >> 10
    place = jnp.where(src >= 0, (src - sender * quota) * LANES + sender, -1)
    state = lax.broadcasted_iota(jnp.int32, (states, LANES), 0)
    which = lax.broadcasted_iota(jnp.int32, (states, LANES), 1)
    labels = jnp.where(
        which == 0, state // rows_block, jnp.where(which == 1, state % rows_block, 0)
    )
    labels = labels.astype(F32).astype(BF)
    for q in range(quota):
        at = lax.broadcasted_iota(jnp.int32, (LANES, states), 0) + q * LANES
        hit_ref[q * LANES : (q + 1) * LANES, :] = one_hot(at == place)
    tags = jnp.transpose(jnp.dot(hit_ref[...], labels, preferred_element_type=F32))
    out_ref[count:, count:] = jnp.zeros((TAGS, width - count), BF)
    out_ref[count:, :count] = tags[:TAGS].astype(BF)
    for cp in loads:
        cp.wait()
    out_ref[:count, :] = jnp.dot(
        hit_ref[...], w_ref[...], preferred_element_type=F32
    ).astype(BF)


def spread_rows(value, out_ref):
    tall = column(value)
    for a in range(value.shape[0]):
        out_ref[a * LANES : (a + 1) * LANES, :] = jnp.broadcast_to(
            tall[:, a : a + 1], (LANES, LANES)
        )


def pack_body(
    orbs, quota, amp_ref, rec_ref, out_any, scale_ref, tile_ref, flat_ref, out_ref, sem_out
):
    rows, width = amp_ref.shape
    tiles = width // LANES
    halves = tiles // orbs
    part = rows // CHUNKS
    groups = part // quota
    spread_rows(rec_ref[...], scale_ref)
    stores = []
    for j in range(CHUNKS):
        here = slice(j * part, (j + 1) * part)
        for t in range(tiles):
            tile_ref[t, here, :] = (
                amp_ref[here, t * LANES : (t + 1) * LANES].astype(F32) * scale_ref[here, :]
            )
        for o in range(orbs):
            for q in range(quota):
                for h in range(halves):
                    piece = tile_ref[o * halves + h, pl.ds(j * part + q, groups, stride=quota), :]
                    at = j * part * tiles + (o * quota + q) * halves + h
                    flat_ref[pl.ds(at, groups, stride=orbs * quota * halves), :] = piece
        to = slice(j * part * tiles, (j + 1) * part * tiles)
        out_ref[to, :] = flat_ref[to, :].astype(BF)
        stores.append(pltpu.make_async_copy(out_ref.at[to], out_any.at[to], sem_out.at[j]))
        stores[j].start()
    for cp in stores:
        cp.wait()


def mix(w, hot_ref, block_ref, owner, out_ref):
    orbs, rows_block, count = hot_ref.shape
    for o in range(orbs):
        spread = jnp.dot(
            w[:, o * rows_block : (o + 1) * rows_block], hot_ref[o], preferred_element_type=F32
        )
        out_ref[:, o * count : (o + 1) * count] = jnp.where(
            owner == block_ref[o, 0:1, :], spread.astype(BF), jnp.zeros((), BF)
        )


def cycle_body(
    quota, here_ref, size_ref, raw_any, far_ref, own_any, after_any, before_any,
    rows_ref, flat_ref, hot_ref, block_ref, owner_ref,
    raw_ref, wide_ref, tag_ref, tags_ref, w_ref, mix_ref, sem_tag, sem_w,
):
    orbs, rows_block, count = hot_ref.shape
    halves = rows_block // LANES
    sources = (own_any, after_any, before_any)
    tag_copies = [
        pltpu.make_async_copy(src.at[count:], tag_ref.at[i], sem_tag.at[i])
        for i, src in enumerate(sources)
    ]
    copies = [
        pltpu.make_async_copy(src.at[:count], w_ref.at[i], sem_w.at[i])
        for i, src in enumerate(sources)
    ]
    raw_copy = pltpu.make_async_copy(raw_any, raw_ref, sem_w.at[3])
    for cp in (*tag_copies, raw_copy, *copies):
        cp.start()
    here = here_ref[0]
    step = orbs * quota * halves
    lane = lax.broadcasted_iota(jnp.int32, (LANES, LANES), 1).astype(F32)
    slot = lax.broadcasted_iota(jnp.int32, (rows_block, count), 0).astype(F32).astype(BF)
    for cp in tag_copies:
        cp.wait()
    tags_ref[2] = far_ref[:, :count]
    for i, s in enumerate((0, 1, 3)):
        tags_ref[s] = tag_ref[i, :, :count]
    sizes = []
    for o in range(orbs):
        tag = tags_ref[(o + orbs - here) % orbs]
        hot_ref[o] = jnp.where(slot == tag[1:2, :], jnp.ones((), BF), jnp.zeros((), BF))
        block_ref[o] = tag
        blocks = tag[0:1, :].astype(F32)
        size = jnp.zeros((1, count), F32)
        for c in range(size_ref.shape[0]):
            live = (size_ref[c] // orbs).astype(F32)
            size = size + jnp.where(blocks == float(c), live, 0.0)
        sizes.append(size)
    sizes = column(jnp.concatenate(sizes, axis=0))
    owners = column(jnp.concatenate([tags_ref[s, 0:1, :].astype(F32) for s in range(orbs)], axis=0))
    owner_ref[...] = jnp.broadcast_to(owners[:, 2:3], (count, LANES)).astype(BF)
    owner = [
        jnp.broadcast_to(owners[:, s : s + 1], (count, LANES)).astype(BF) for s in range(orbs)
    ]
    for cp in (raw_copy, *copies):
        cp.wait()
    wide_ref[...] = raw_ref[...].astype(F32)
    mix(w_ref.at[0], hot_ref, block_ref, owner[0][:, 0:1], mix_ref.at[0])
    for o in range(orbs):
        for q in range(quota):
            row = o * count + q * LANES
            size = sizes[q * LANES : (q + 1) * LANES, o : o + 1]
            for h in range(halves):
                piece = wide_ref[pl.ds((o * quota + q) * halves + h, LANES, stride=step), :]
                rows_ref[row : row + LANES, h * LANES : (h + 1) * LANES] = jnp.where(
                    lane + float(h * LANES) < size, piece, 0.0
                ).astype(BF)
    mix(w_ref.at[1], hot_ref, block_ref, owner[1][:, 0:1], mix_ref.at[1])
    mix(w_ref.at[2], hot_ref, block_ref, owner[3][:, 0:1], mix_ref.at[2])
    for i, s in enumerate((0, 1, 3)):
        scatter(quota, (here + s) % orbs, step, mix_ref[i], rows_ref, flat_ref)


def scatter(quota, to, step, mix, rows_ref, flat_ref):
    halves = rows_ref.shape[1] // LANES
    done = jnp.dot(mix, rows_ref[...], preferred_element_type=F32)
    for q in range(quota):
        for h in range(halves):
            flat_ref[pl.ds((to * quota + q) * halves + h, LANES, stride=step), :] = done[
                q * LANES : (q + 1) * LANES, h * LANES : (h + 1) * LANES
            ]


def close_body(
    quota, here_ref, lo_any, hi_ref, hot_ref, block_ref, owner_ref, rows_ref, flat_in,
    out_ref, flat_ref, lo_ref, mix_ref, sem,
):
    orbs, rows_block, _ = hot_ref.shape
    half = lo_ref.shape[0]
    step = orbs * quota * (rows_block // LANES)
    load = pltpu.make_async_copy(lo_any, lo_ref, sem)
    load.start()
    mix(hi_ref, hot_ref, block_ref, owner_ref[half:, 0:1], mix_ref.at[half:])
    load.wait()
    mix(lo_ref, hot_ref, block_ref, owner_ref[:half, 0:1], mix_ref.at[:half])
    scatter(quota, (here_ref[0] + 2) % orbs, step, mix_ref[...], rows_ref, flat_ref)
    out_ref[...] = flat_ref[...].astype(BF)


def finish_body(
    orbs, quota, raw_ref, amp_ref, rec_ref, den_ref, out_any,
    scale_ref, flat_ref, tile_ref, out_ref, sem_out,
):
    rows, width = amp_ref.shape
    tiles = width // LANES
    halves = tiles // orbs
    part = rows // CHUNKS
    groups = part // quota
    spread_rows(rec_ref[...] / den_ref[...], scale_ref)
    stores = []
    for j in range(CHUNKS):
        here = slice(j * part, (j + 1) * part)
        to = slice(j * part * tiles, (j + 1) * part * tiles)
        flat_ref[to, :] = raw_ref[to, :].astype(F32)
        for o in range(orbs):
            for q in range(quota):
                for h in range(halves):
                    at = j * part * tiles + (o * quota + q) * halves + h
                    piece = flat_ref[pl.ds(at, groups, stride=orbs * quota * halves), :]
                    tile_ref[o * halves + h, pl.ds(j * part + q, groups, stride=quota), :] = piece
        for t in range(tiles):
            cols = slice(t * LANES, (t + 1) * LANES)
            move = scale_ref[here, :] * tile_ref[t, here, :]
            out_ref[here, cols] = (amp_ref[here, cols].astype(F32) + move).astype(BF)
        stores.append(pltpu.make_async_copy(out_ref.at[here], out_any.at[here], sem_out.at[j]))
        stores[j].start()
    for cp in stores:
        cp.wait()


def pick(pair_source, interaction, quota):
    blocks, rows_block, width = interaction.shape
    count = quota * LANES
    states = blocks * rows_block
    return call(
        functools.partial(pick_body, quota),
        pltpu.VMEM((count + TAGS, width), BF),
        [ANY, ANY],
        VM,
        [
            pltpu.VMEM((blocks, rows_block), jnp.int32),
            pltpu.VMEM((states, width), BF),
            pltpu.VMEM((count, states), BF),
            pltpu.SemaphoreType.DMA,
            pltpu.SemaphoreType.DMA((blocks,)),
        ],
        name="pick",
    )(apart(pair_source), apart(interaction.reshape(states, width)))


def pack(amplitudes, recoupling, orbs, quota):
    rows, width = amplitudes.shape
    tiles = width // LANES
    return call(
        functools.partial(pack_body, orbs, quota),
        pltpu.HBM((rows * tiles, LANES), BF),
        [VM, VM],
        ANY,
        [
            pltpu.VMEM((rows, LANES), F32),
            pltpu.VMEM((tiles, rows, LANES), F32),
            pltpu.VMEM((rows * tiles, LANES), F32),
            pltpu.VMEM((rows * tiles, LANES), BF),
            pltpu.SemaphoreType.DMA((CHUNKS,)),
        ],
        name="pack",
    )(near(amplitudes), recoupling.reshape(rows // LANES, LANES))


def cycle(here, sizes, raw, far, own, after, before, quota):
    count = quota * LANES
    width = own.shape[1]
    return call(
        functools.partial(cycle_body, quota),
        (
            pltpu.VMEM((4 * count, 2 * LANES), BF),
            pltpu.VMEM(raw.shape, F32),
            pltpu.VMEM((4, 2 * LANES, count), BF),
            pltpu.VMEM((4, TAGS, count), BF),
            pltpu.VMEM((count, LANES), BF),
        ),
        [SM, SM, ANY, VM] + [ANY] * 3,
        (VM,) * 5,
        [
            pltpu.VMEM(raw.shape, BF),
            pltpu.VMEM(raw.shape, F32),
            pltpu.VMEM((3, TAGS, width), BF),
            pltpu.VMEM((4, TAGS, count), BF),
            pltpu.VMEM((3, count, width), BF),
            pltpu.VMEM((3, count, 4 * count), BF),
            pltpu.SemaphoreType.DMA((3,)),
            pltpu.SemaphoreType.DMA((4,)),
        ],
        name="cycle",
    )(here, sizes, raw, far, own, after, before)


def close(here, lo, hi, hot, block, owner, rows, flat, quota):
    count = quota * LANES
    out, _ = call(
        functools.partial(close_body, quota),
        (pltpu.VMEM(flat.shape, BF), pltpu.VMEM(flat.shape, F32)),
        [SM, ANY] + [VM] * 6,
        (VM, VM),
        [
            pltpu.VMEM(lo.shape, BF),
            pltpu.VMEM((count, 4 * count), BF),
            pltpu.SemaphoreType.DMA,
        ],
        input_output_aliases={7: 1},
        name="close",
    )(here, apart(lo), near(hi), near(hot), near(block), near(owner), near(rows), near(flat))
    return out


def finish(raw, amplitudes, recoupling, denominators, orbs, quota):
    rows, width = amplitudes.shape
    tiles = width // LANES
    return call(
        functools.partial(finish_body, orbs, quota),
        jax.ShapeDtypeStruct((rows, width), BF),
        [VM, VM, VM, VM],
        ANY,
        [
            pltpu.VMEM((rows, LANES), F32),
            pltpu.VMEM((rows * tiles, LANES), F32),
            pltpu.VMEM((tiles, rows, LANES), F32),
            pltpu.VMEM((rows, width), BF),
            pltpu.SemaphoreType.DMA((CHUNKS,)),
        ],
        name="finish",
    )(
        near(raw), near(amplitudes),
        recoupling.reshape(rows // LANES, LANES), denominators.reshape(rows // LANES, LANES),
    )


def shards(
    amplitudes, recoupling, denominators, interaction, pair_source, return_slot, channel_sizes
):
    chan_count = lax.axis_size("chan")
    orbs = lax.axis_size("orb")
    row_count, _ = amplitudes.shape
    quota = row_count // chan_count
    count = quota * LANES
    early = count * 23 // 40
    halves = pair_source.shape[1] // LANES
    peers = chan_count * orbs

    def shift(x, by):
        return lax.ppermute(x, "orb", [(i, (i + by) % orbs) for i in range(orbs)])

    def exchange(x):
        x = x.reshape(peers, quota, halves, LANES)
        x = lax.all_to_all(x, BOTH, split_axis=0, concat_axis=0, tiled=True)
        return x.reshape(peers * quota * halves, LANES)

    own = pick(pair_source, interaction, quota)
    after = shift(own, -1)
    before = shift(own, 1)
    outgoing, _ = lax.optimization_barrier((pack(amplitudes, recoupling, orbs, quota), own))
    raw = exchange(outgoing)
    far = shift(own[count:], 2)
    lo = shift(after[:early], -1)
    hi = shift(before[early:count], 1)
    here = lax.axis_index("orb").astype(jnp.int32).reshape(1)
    rows, flat, hot, block, owner = cycle(
        here, channel_sizes, raw, far, own, after, before, quota
    )
    back = close(here, lo, hi, hot, block, owner, rows, flat, quota)
    returned = exchange(back)
    return finish(returned, amplitudes, recoupling, denominators, orbs, quota)


def solution(mesh):
    in_specs = (
        P(("chan", "orb"), None),
        P(("chan", "orb")),
        P(("chan", "orb")),
        P("chan", "orb", None),
        P("chan", "orb"),
        P(("chan", "orb")),
        P("chan"),
    )
    out_specs = P(("chan", "orb"), None)
    return jax.shard_map(
        shards, mesh=mesh, in_specs=in_specs, out_specs=out_specs, check_vma=False
    )
```
